128 devices in a mesh: lon: 32 (over z_lo, y, x), lat: 4 (over z_hi, core).
Axes of the slice: x: 4, y: 4, z: 4 (z_hi: 2, z_lo: 2; z = z_hi * 2 + z_lo), core: 2. Of those that a mesh axis runs over, the one named last changes fastest.
Arguments:
- tokens: bfloat16 [6, 288, 768, 192], P(None, 'lat', 'lon'), may hold values from -6 to 6
- obs_values: bfloat16 [262144, 256], P(('lon', 'lat')), may hold values from -6 to 6
- obs_dest: int32 [262144], P(('lon', 'lat')), may hold values from 0 to 127, as said below
- obs_cell: int32 [262144], P(('lon', 'lat')), may hold values from 0 to 10367
- obs_count: int32 [128], P(('lon', 'lat')), may hold values from 1365 to 2048, as said below
- w_obs: bfloat16 [256, 192], replicated, may hold values from -0.375 to 0.375
- ln1_gain: float32 [192], replicated, may hold values from 0.1 to 1.9
- w_qkv: bfloat16 [192, 576], replicated, may hold values from -0.4375 to 0.4375
- position_bias: float32 [6, 144, 144], replicated, may hold values from -4 to 400
- w_proj: bfloat16 [192, 192], replicated, may hold values from -0.4375 to 0.4375
- ln2_gain: float32 [192], replicated, may hold values from 0.1 to 1.9
- w_up: bfloat16 [192, 768], replicated, may hold values from -0.4375 to 0.4375
- w_down: bfloat16 [768, 192], replicated, may hold values from -0.21875 to 0.21875
Outputs:
- block_out: bfloat16 [6, 288, 768, 192], P(None, 'lat', 'lon')
The draws below stay inside these ranges and needn't reach their ends.
Inputs may be any that keep to these rules, and one draw needn't show every extreme that they name: `obs_dest`: the tile owning a row, numbered lon index * 4 + lat index; among the live rows of one device no tile is named more than 32 times, and in every draw one tile is named exactly 32 times by the live rows of every device. `obs_cell`: a cell of the owning tile, numbered (level * 72 + row) * 24 + column. The live rows of device s are the first obs_count[s] rows of its block; the others are padding.
All inputs are finite; a program needn't handle non-finite values.
Results may differ from the reference program's by a relative error of at most 0.01.
Values may be sent and summed in bfloat16 or wider, within the bound.
A program may use at most 128 MiB of HBM per device.

```python
import math
import jax
import jax.numpy as jnp
from jax import lax

D = 192
HEADS = 6
HID = 768
F_OBS = 256
WZ = 2
WLAT = 6
WLON = 12
NZ = 6
LA = 72
LO = 24
OBS_DEV = 2048
WIN = 144
NLAT = 288
NLON = 768
TOK_DEV = 10368
CAP = 32
N_LAT = 4
DEVICES = 128


def routing(key):
    base = jax.random.fold_in(key, 5)
    hot_key, count_key, rest_key = jax.random.split(base, 3)
    hottest = jax.random.randint(hot_key, (), 0, DEVICES)
    counts = jax.random.randint(count_key, (DEVICES,), 2 * OBS_DEV // 3, OBS_DEV + 1)
    pool_ids = jnp.arange(DEVICES * CAP, dtype=jnp.int32) // CAP

    def one_source(source_key, count_live):
        first_key, second_key = jax.random.split(source_key)
        mixed_ids = jax.random.permutation(first_key, pool_ids)
        ranking = jnp.argsort(jnp.where(mixed_ids == hottest, 0, 1), stable=True)
        listed = mixed_ids[ranking][:OBS_DEV]
        position = jnp.arange(OBS_DEV, dtype=jnp.int32)
        random_keys = jax.random.randint(second_key, (OBS_DEV,), 0, 2 ** 30 // OBS_DEV) * OBS_DEV + position
        ordering = jnp.where(position < count_live, random_keys, 2 ** 30 + position)
        placed = jnp.argsort(ordering, stable=True)
        return jnp.zeros((OBS_DEV,), jnp.int32).at[placed].set(listed)
    dest_ids = jax.vmap(one_source)(jax.random.split(rest_key, DEVICES), counts)
    return (dest_ids, counts.astype(jnp.int32))


def draw_obs_dest(key, part):
    return routing(key)[0].reshape(-1)


def draw_obs_count(key, part):
    return routing(key)[1]


def draw_position_bias(key, part):
    base = jax.random.fold_in(key, 11)
    first = jax.random.fold_in(base, 0)
    table_shape = (HEADS, WIN, WIN)
    table = jnp.clip(jax.random.normal(first, table_shape, jnp.float32), -4.0, 4.0)
    return table


def with_ends(array, stream_key, low, top_value):
    spot = [jax.random.randint(jax.random.fold_in(stream_key, axis), (), 0, length) for axis, length in enumerate(array.shape)]
    main_axis = array.shape.index(max(array.shape))
    beside = spot[:main_axis] + [(spot[main_axis] + 1) % array.shape[main_axis]] + spot[main_axis + 1:]
    return array.at[tuple(spot)].set(low).at[tuple(beside)].set(top_value)


def steps_of(own_key, dims, cuts, smallest, high):
    factor_of, own = 1.0, jax.random.fold_in(own_key, 6)
    for dim, shards_of in cuts:
        steps = jnp.exp(jax.random.uniform(jax.random.fold_in(own, dim), (shards_of,), jnp.float32, smallest / len(cuts), high / len(cuts)))
        factor_of = factor_of * jnp.repeat(steps, dims[dim] // shards_of).reshape([-1 if axis == dim else 1 for axis in range(len(dims))])
    return factor_of


def gaussian(key, dims, deviation, limit, shards=(), held_as=jnp.bfloat16):
    level = steps_of(key, dims, shards, -0.22, 0.18) if shards else 1.0
    array = jax.random.normal(key, dims, jnp.float32) * deviation * level
    return jnp.minimum(jnp.maximum(array, -limit), limit).astype(held_as)


def setup_inputs(seed: int = 0) -> dict:
    arg_keys = jax.random.split(jax.random.key(seed), 14)
    tokens = gaussian(arg_keys[0], (NZ, NLAT, NLON, D), 1.0, 6.0, ((1, 4), (2, 32)))
    obs_values = gaussian(arg_keys[1], (DEVICES * OBS_DEV, F_OBS), 1.0, 6.0, ((0, 128),))
    obs_dest = draw_obs_dest(jax.random.fold_in(arg_keys[13], 71), 0)
    obs_cell = with_ends(jax.random.randint(arg_keys[3], (DEVICES * OBS_DEV,), 0, TOK_DEV), jax.random.fold_in(arg_keys[3], 1), 0, TOK_DEV - 1).astype(jnp.int32)
    obs_count = draw_obs_count(jax.random.fold_in(arg_keys[13], 71), 0)
    w_obs = gaussian(arg_keys[5], (F_OBS, D), F_OBS ** -0.5, 0.375)
    ln1_gain = jnp.clip(1.0 + 0.18 * jax.random.normal(arg_keys[6], (D,), jnp.float32), 0.1, 1.9)
    w_qkv = gaussian(arg_keys[7], (D, 3 * D), D ** -0.5, 0.4375)
    position_bias = draw_position_bias(jax.random.fold_in(arg_keys[13], 71), 0)
    w_proj = gaussian(arg_keys[9], (D, D), D ** -0.5, 0.4375)
    ln2_gain = jnp.clip(1.0 + 0.18 * jax.random.normal(arg_keys[10], (D,), jnp.float32), 0.1, 1.9)
    w_up = gaussian(arg_keys[11], (D, HID), D ** -0.5, 0.4375)
    w_down = gaussian(arg_keys[12], (HID, D), HID ** -0.5, 0.21875)
    return dict(tokens=tokens, obs_values=obs_values, obs_dest=obs_dest, obs_cell=obs_cell, obs_count=obs_count, w_obs=w_obs, ln1_gain=ln1_gain, w_qkv=w_qkv, position_bias=position_bias, w_proj=w_proj, ln2_gain=ln2_gain, w_up=w_up, w_down=w_down)


def layer_norm(inputs, gain):
    values32 = inputs.astype(jnp.float32)
    average = lax.optimization_barrier(jnp.mean(values32, axis=-1, keepdims=True))
    centered = values32 - average
    variance = lax.optimization_barrier(jnp.mean(centered * centered, axis=-1, keepdims=True))
    return centered * lax.rsqrt(variance + 1e-05) * gain

def to_windows(grid):
    levels, lat_rows, lon_cols = grid.shape[:3]
    trailing = grid.shape[3:]
    shaped = grid.reshape((levels // WZ, WZ, lat_rows // WLAT, WLAT, lon_cols // WLON, WLON) + trailing)
    axes_order = (2, 0, 4, 1, 3, 5) + tuple(range(6, 6 + len(trailing)))
    return shaped.transpose(axes_order).reshape((lat_rows // WLAT, levels // WZ * (lon_cols // WLON), WZ * WLAT * WLON) + trailing)

def from_windows(windows, levels, lat_rows, lon_cols):
    trailing = windows.shape[3:]
    shaped = windows.reshape((lat_rows // WLAT, levels // WZ, lon_cols // WLON, WZ, WLAT, WLON) + trailing)
    axes_order = (1, 3, 0, 4, 2, 5) + tuple(range(6, 6 + len(trailing)))
    return shaped.transpose(axes_order).reshape((levels, lat_rows, lon_cols) + trailing)

def attend_windows(block, grouped, bias, ln1_gain, w_qkv, w_proj):
    amount, win_size, features = block.shape
    heads = bias.shape[0]
    head_dim = features // heads
    normed = layer_norm(block, ln1_gain).astype(jnp.bfloat16)
    qkv_rows = jnp.dot(normed.reshape(-1, features), w_qkv, preferred_element_type=jnp.float32).astype(jnp.bfloat16)
    qkv_rows = qkv_rows.reshape(amount, win_size, 3, heads, head_dim)
    query = qkv_rows[:, :, 0].astype(jnp.float32)
    key_rows = qkv_rows[:, :, 1].astype(jnp.float32)
    value_rows = qkv_rows[:, :, 2].astype(jnp.float32)
    scores = jnp.einsum('wqhc,wkhc->whqk', query, key_rows)
    scores = scores * (1.0 / math.sqrt(head_dim)) + bias[None]
    allowed = grouped[:, None, :, None] == grouped[:, None, None, :]
    scores = jnp.where(allowed, scores, -1e+30)
    highest = lax.optimization_barrier(jnp.max(scores, axis=-1, keepdims=True))
    weights = jnp.exp(scores - highest)
    prob_bf = (weights / lax.optimization_barrier(jnp.sum(weights, axis=-1, keepdims=True))).astype(jnp.bfloat16)
    context = jnp.einsum('whqk,wkhc->wqhc', prob_bf.astype(jnp.float32), value_rows).astype(jnp.bfloat16)
    mixed_f = jnp.dot(context.reshape(-1, features), w_proj, preferred_element_type=jnp.float32)
    result = (block.reshape(-1, features).astype(jnp.float32) + mixed_f).astype(jnp.bfloat16)
    return result.reshape(amount, win_size, features)

def window_pass(shifted, first_row, total_rows, bias, ln1_gain, w_qkv, w_proj):
    levels, lat_rows, lon_cols = shifted.shape[:3]
    half_z = WZ // 2
    half_lat = WLAT // 2
    rolled = jnp.roll(shifted, -half_z, axis=0)
    anchor = first_row + jnp.arange(lat_rows, dtype=jnp.int32)
    lat_flag = (anchor >= 0) & (anchor < half_lat) | (anchor >= total_rows)
    level_flag = jnp.arange(levels, dtype=jnp.int32) >= levels - half_z
    grouped = 2 * lat_flag.astype(jnp.int32)[None, :, None] + level_flag.astype(jnp.int32)[:, None, None]
    grouped = jnp.broadcast_to(grouped, (levels, lat_rows, lon_cols))
    windows = to_windows(rolled)
    labels = to_windows(grouped[..., None])[..., 0]
    attended = lax.map(lambda operands: attend_windows(operands[0], operands[1], bias, ln1_gain, w_qkv, w_proj), (windows, labels))
    return jnp.roll(from_windows(attended, levels, lat_rows, lon_cols), half_z, axis=0)

def feed_forward(rows_in, ln2_gain, w_up, w_down):
    normed = layer_norm(rows_in, ln2_gain).astype(jnp.bfloat16)
    hidden = jax.nn.gelu(jnp.dot(normed, w_up, preferred_element_type=jnp.float32), approximate=False).astype(jnp.bfloat16)
    return (rows_in.astype(jnp.float32) + jnp.dot(hidden, w_down, preferred_element_type=jnp.float32)).astype(jnp.bfloat16)

def feed_grid(grid, ln2_gain, w_up, w_down):
    blocks = grid.reshape(grid.shape[1] // WLAT, -1, grid.shape[3])
    result = lax.map(lambda rows_in: feed_forward(rows_in, ln2_gain, w_up, w_down), blocks)
    return result.reshape(grid.shape)

def reference(tokens, obs_values, obs_dest, obs_cell, obs_count, w_obs, ln1_gain, w_qkv, position_bias, w_proj, ln2_gain, w_up, w_down):
    embedded = jnp.dot(obs_values, w_obs, preferred_element_type=jnp.float32).astype(jnp.bfloat16)
    row_ids = jnp.arange(DEVICES * OBS_DEV, dtype=jnp.int32)
    is_live = row_ids % OBS_DEV < jnp.repeat(obs_count, OBS_DEV)
    lon_tile = obs_dest // N_LAT
    lat_tile = obs_dest % N_LAT
    level_ids = obs_cell // (LA * LO)
    lat_ids = lat_tile * LA + obs_cell // LO % LA
    lon_ids = lon_tile * LO + obs_cell % LO
    terms = jnp.where(is_live[:, None], embedded.astype(jnp.float32), 0.0)
    obs_field = jnp.zeros((NZ, NLAT, NLON, D), jnp.float32).at[level_ids, lat_ids, lon_ids].add(terms)
    stream = (tokens.astype(jnp.float32) + obs_field).astype(jnp.bfloat16)
    half_lat = WLAT // 2
    half_lon = WLON // 2
    shifted = jnp.roll(stream, (-half_lat, -half_lon), axis=(1, 2))
    attended = window_pass(shifted, half_lat, NLAT, position_bias, ln1_gain, w_qkv, w_proj)
    result = feed_grid(attended, ln2_gain, w_up, w_down)
    return jnp.roll(result, (half_lat, half_lon), axis=(1, 2))
```

```python
import math

import jax
import jax.numpy as jnp
import numpy as np
from jax import lax
from jax.experimental import pallas as pl
from jax.experimental.pallas import tpu as pltpu
from jax.sharding import PartitionSpec as P

WZ = 2
WLAT = 6
WLON = 12
F32=jnp.float32; BF=jnp.bfloat16
WIN=144; D=192; HEADS=6; HD=32
NT=(((1,),(1,)),((),()))
LOG2E=math.log2(math.e)

def dot(a,b): return jnp.dot(a,b,preferred_element_type=F32)
def dot_nt(a,b): return lax.dot_general(a,b,NT,preferred_element_type=F32)

def norm(x, gain):
    mean=jnp.mean(x,axis=-1,keepdims=True)
    c=x-mean
    var=jnp.mean(c*c,axis=-1,keepdims=True)
    return (c*lax.rsqrt(var+1e-5)*gain).astype(BF)

def gelu(x):
    h=0.5*x
    return h+h*lax.erf(x*np.float32(math.sqrt(0.5)))

def head_mask(shape, h, width=HD):
    lane=lax.broadcasted_iota(jnp.int32,shape,len(shape)-1)
    return (lane>=h*width)&(lane<(h+1)*width)

GROUPS=((0,4,0,128),(4,2,128,64))

def kernel(edge_ref, x_ref, bias_ref, g1_ref, wqkv_ref, wp_ref, g2_ref, wup_ref, wdnt_ref, o_ref, xs, s_ref, p_ref, ctx_ref):
    band=pl.program_id(0)
    lat_edge=jnp.where(band==pl.num_programs(0)-1, edge_ref[0], 0)
    zero=jnp.zeros((),BF)
    def pair(k,_):
        lvls=(2*k+1, lax.rem(2*k+2,6))
        for i in range(2):
            for r in range(6):
                row=x_ref[lvls[i], r].astype(F32)
                for w in range(2):
                    base=w*WIN+(i*6+r)*12
                    xs[base:base+12,:]=row[w*12:w*12+12]
        lvl_edge=(k==2).astype(jnp.int32)
        var=2*lat_edge+lvl_edge
        n1=norm(xs[...],g1_ref[...])
        q_all=(dot(n1,wqkv_ref[:,0:256])*np.float32(LOG2E/math.sqrt(HD))).astype(BF)
        k_all=dot(n1,wqkv_ref[:,256:512]).astype(BF)
        v_all=dot(n1,wqkv_ref[:,512:768]).astype(BF)
        for w in range(2):
            sl=slice(w*WIN,(w+1)*WIN)
            for h0,nh,l0,ln in GROUPS:
                qg=q_all[sl,l0:l0+128]; kg=k_all[sl,l0:l0+128]
                qs=jnp.concatenate([jnp.where(head_mask((WIN,128),h),qg,zero) for h in range(nh)],axis=0)
                s_ref[w,h0*WIN:(h0+nh)*WIN,:]=dot_nt(qs,kg)
        for w in range(2):
            sl=slice(w*WIN,(w+1)*WIN)
            ls=[]
            for h in range(HEADS):
                s=s_ref[w,h*WIN:(h+1)*WIN,:]+bias_ref[var,h*WIN:(h+1)*WIN,:]
                m=jnp.max(s,axis=-1,keepdims=True)
                p=jnp.exp2(s-m)
                ls.append(jnp.sum(p,axis=-1,keepdims=True))
                p_ref[w,h*WIN:(h+1)*WIN,:]=p.astype(BF)
            for h0,nh,l0,ln in GROUPS:
                o=dot(p_ref[w,h0*WIN:(h0+nh)*WIN,:],v_all[sl,l0:l0+128])
                c=o[:WIN]; l=ls[h0]*jnp.ones((1,128),F32)
                for h in range(1,nh):
                    mk=head_mask((WIN,128),h)
                    c=jnp.where(mk,o[h*WIN:(h+1)*WIN],c)
                    l=jnp.where(mk,ls[h0+h],l)
                ctx_ref[sl,l0:l0+128]=(c*(1.0/l)).astype(BF)
        att=(xs[...]+dot(ctx_ref[:,:D],wp_ref[...])).astype(BF).astype(F32)
        n2=norm(att,g2_ref[...])
        acc=att
        for j in range(3):
            hid=gelu(dot(n2,wup_ref[:,j*256:(j+1)*256])).astype(BF)
            acc=acc+dot_nt(hid,wdnt_ref[:,j*256:(j+1)*256])
        xs[...]=acc
        for i in range(2):
            for r in range(6):
                for w in range(2):
                    base=w*WIN+(i*6+r)*12
                    o_ref[lvls[i], r, w*12:w*12+12,:]=xs[base:base+12,:].astype(BF)
        return 0
    lax.fori_loop(0,3,pair,0)

def prep_bias(position_bias):
    b=position_bias*np.float32(LOG2E)
    lvl=np.arange(WIN)//72; row=np.arange(WIN)//12%6
    outs=[]
    for le in range(2):
        for ve in range(2):
            g=2*le*(row>=3)+ve*lvl
            outs.append((g[:,None]!=g[None,:]).astype(np.float32)*np.float32(-1e30))
    return (b[None]+jnp.asarray(np.stack(outs))[:,None]).reshape(4,HEADS*WIN,WIN)

def compute(shifted, lat_edge, position_bias, g1, wqkv, wp, g2, wup, wdn):
    bias=prep_bias(position_bias)
    wq=jnp.pad(wqkv.reshape(D,3,D),((0,0),(0,0),(0,64))).reshape(D,768)
    full=lambda *s: pl.BlockSpec(s,lambda i:(0,)*len(s),pipeline_mode=pl.Buffered(1))
    return pl.pallas_call(
        kernel, grid=(12,),
        in_specs=[pl.BlockSpec(memory_space=pltpu.SMEM),
          pl.BlockSpec((6,6,24,D),lambda i:(0,i,0,0)),
          full(4,HEADS*WIN,WIN),full(1,D),full(D,768),full(D,D),full(1,D),full(D,768),full(D,768)],
        out_specs=pl.BlockSpec((6,6,24,D),lambda i:(0,i,0,0)),
        out_shape=jax.ShapeDtypeStruct((6,72,24,D),BF),
        scratch_shapes=[pltpu.VMEM((2*WIN,D),F32),pltpu.VMEM((2,HEADS*WIN,WIN),F32),pltpu.VMEM((2,HEADS*WIN,WIN),BF),pltpu.VMEM((2*WIN,256),BF)],
        compiler_params=pltpu.CompilerParams(vmem_limit_bytes=56<<20),
    )(lat_edge,shifted,bias,g1.reshape(1,D),wq,wp,g2.reshape(1,D),wup,wdn.T)


def passed_along(block, axis, distance):
    devices = range(lax.axis_size(axis))
    route = [((i - distance) % len(devices), i) for i in devices]
    return lax.ppermute(block, axis, route)


def on_device(
    tokens,
    obs_values,
    obs_dest,
    obs_cell,
    obs_count,
    w_obs,
    ln1_gain,
    w_qkv,
    position_bias,
    w_proj,
    ln2_gain,
    w_up,
    w_down,
):
    levels, lat_rows, lon_cols, features = tokens.shape
    lon_count = lax.axis_size("lon")
    lat_count = lax.axis_size("lat")
    devices = lon_count * lat_count
    row_count = obs_values.shape[0]
    capacity = 2 * row_count // devices
    position = jnp.arange(row_count, dtype=jnp.int32)
    is_live = position < obs_count[0]
    matches = (
        (obs_dest[:, None] == jnp.arange(devices, dtype=jnp.int32)[None, :]) & is_live[:, None]
    ).astype(jnp.int32)
    earlier = jnp.cumsum(matches, axis=0) - matches
    slot_ids = jnp.sum(earlier * matches, axis=1)
    targets = jnp.where(is_live, obs_dest * capacity + slot_ids, devices * capacity)
    cell_ids = jnp.zeros((devices * capacity,), jnp.int32).at[targets].set(obs_cell, mode="drop")
    payload = jnp.dot(obs_values, w_obs, preferred_element_type=jnp.float32).astype(jnp.bfloat16)
    buffer = (
        jnp.zeros((devices * capacity, payload.shape[1]), jnp.bfloat16)
        .at[targets]
        .set(payload, mode="drop")
    )
    received, got_cells = (
        lax.all_to_all(buffer, ("lon", "lat"), split_axis=0, concat_axis=0, tiled=True),
        lax.all_to_all(cell_ids, ("lon", "lat"), split_axis=0, concat_axis=0, tiled=True),
    )
    obs_field = (
        jnp.zeros((levels * lat_rows * lon_cols, features), jnp.float32)
        .at[got_cells]
        .add(received.astype(jnp.float32))
    )
    stream = (tokens.astype(jnp.float32) + obs_field.reshape(tokens.shape)).astype(jnp.bfloat16)
    half_lat = WLAT // 2
    half_lon = WLON // 2
    lat_index = lax.axis_index("lat")
    arrived = passed_along(stream[:, :, :half_lon], "lon", -1)
    widened = jnp.concatenate([stream[:, :, half_lon:], arrived], axis=2)
    arrived = passed_along(widened[:, :half_lat], "lat", -1)
    shifted = jnp.concatenate([widened[:, half_lat:], arrived], axis=1)
    edge = (lat_index == lat_count - 1).astype(jnp.int32).reshape(1)
    result = compute(
        shifted, edge, position_bias, ln1_gain, w_qkv, w_proj, ln2_gain, w_up, w_down
    )
    arrived = passed_along(result[:, lat_rows - half_lat :], "lat", 1)
    widened = jnp.concatenate([arrived, result[:, : lat_rows - half_lat]], axis=1)
    arrived = passed_along(widened[:, :, lon_cols - half_lon :], "lon", 1)
    return jnp.concatenate([arrived, widened[:, :, : lon_cols - half_lon]], axis=2)


def solution(mesh):
    in_specs = (
        P(None, "lat", "lon", None),
        P(("lon", "lat"), None),
        P(("lon", "lat")),
        P(("lon", "lat")),
        P(("lon", "lat")),
        P(),
        P(),
        P(),
        P(),
        P(),
        P(),
        P(),
        P(),
    )
    out_specs = P(None, "lat", "lon", None)
    return jax.shard_map(
        on_device, mesh=mesh, in_specs=in_specs, out_specs=out_specs, check_vma=False
    )
```

```python
import math

import jax
import jax.numpy as jnp
import numpy as np
from jax import lax
from jax.experimental import pallas as pl
from jax.experimental.pallas import tpu as pltpu
from jax.sharding import PartitionSpec as P

WZ = 2
WLAT = 6
WLON = 12
F32=jnp.float32; BF=jnp.bfloat16
WIN=144; D=192; HEADS=6; HD=32
NT=(((1,),(1,)),((),()))
LOG2E=math.log2(math.e)

def dot(a,b): return jnp.dot(a,b,preferred_element_type=F32)
def dot_nt(a,b): return lax.dot_general(a,b,NT,preferred_element_type=F32)

def norm(x, gain):
    mean=jnp.mean(x,axis=-1,keepdims=True)
    c=x-mean
    var=jnp.mean(c*c,axis=-1,keepdims=True)
    return (c*lax.rsqrt(var+1e-5)*gain).astype(BF)

def gelu(x):
    h=0.5*x
    return h+h*lax.erf(x*np.float32(math.sqrt(0.5)))

def head_mask(shape, h, width=HD):
    lane=lax.broadcasted_iota(jnp.int32,shape,len(shape)-1)
    return (lane>=h*width)&(lane<(h+1)*width)

GROUPS=((0,4,0,128),(4,2,128,64))

def kernel(edge_ref, x_ref, bias_ref, g1_ref, wqkv_ref, wp_ref, g2_ref, wup_ref, wdnt_ref, o_ref, xs, s_ref, p_ref, ctx_ref):
    band=pl.program_id(0)
    lat_edge=jnp.where(band==pl.num_programs(0)-1, edge_ref[0], 0)
    zero=jnp.zeros((),BF)
    def pair(k,_):
        lvls=(2*k+1, lax.rem(2*k+2,6))
        for i in range(2):
            for r in range(6):
                row=x_ref[lvls[i], r].astype(F32)
                for w in range(2):
                    base=w*WIN+(i*6+r)*12
                    xs[base:base+12,:]=row[w*12:w*12+12]
        lvl_edge=(k==2).astype(jnp.int32)
        var=2*lat_edge+lvl_edge
        n1=norm(xs[...],g1_ref[...])
        q_all=(dot(n1,wqkv_ref[:,0:256])*np.float32(LOG2E/math.sqrt(HD))).astype(BF)
        k_all=dot(n1,wqkv_ref[:,256:512]).astype(BF)
        v_all=dot(n1,wqkv_ref[:,512:768]).astype(BF)
        for w in range(2):
            sl=slice(w*WIN,(w+1)*WIN)
            for h0,nh,l0,ln in GROUPS:
                qg=q_all[sl,l0:l0+128]; kg=k_all[sl,l0:l0+128]
                qs=jnp.concatenate([jnp.where(head_mask((WIN,128),h),qg,zero) for h in range(nh)],axis=0)
                s_ref[w,h0*WIN:(h0+nh)*WIN,:]=dot_nt(qs,kg)
        for w in range(2):
            sl=slice(w*WIN,(w+1)*WIN)
            ls=[]
            for h in range(HEADS):
                s=s_ref[w,h*WIN:(h+1)*WIN,:]+bias_ref[var,h*WIN:(h+1)*WIN,:]
                m=jnp.max(s,axis=-1,keepdims=True)
                p=jnp.exp2(s-m)
                ls.append(jnp.sum(p,axis=-1,keepdims=True))
                p_ref[w,h*WIN:(h+1)*WIN,:]=p.astype(BF)
            for h0,nh,l0,ln in GROUPS:
                o=dot(p_ref[w,h0*WIN:(h0+nh)*WIN,:],v_all[sl,l0:l0+128])
                c=o[:WIN]; l=ls[h0]*jnp.ones((1,128),F32)
                for h in range(1,nh):
                    mk=head_mask((WIN,128),h)
                    c=jnp.where(mk,o[h*WIN:(h+1)*WIN],c)
                    l=jnp.where(mk,ls[h0+h],l)
                ctx_ref[sl,l0:l0+128]=(c*(1.0/l)).astype(BF)
        att=(xs[...]+dot(ctx_ref[:,:D],wp_ref[...])).astype(BF).astype(F32)
        n2=norm(att,g2_ref[...])
        acc=att
        for j in range(3):
            hid=gelu(dot(n2,wup_ref[:,j*256:(j+1)*256])).astype(BF)
            acc=acc+dot_nt(hid,wdnt_ref[:,j*256:(j+1)*256])
        xs[...]=acc
        for i in range(2):
            for r in range(6):
                for w in range(2):
                    base=w*WIN+(i*6+r)*12
                    o_ref[lvls[i], r, w*12:w*12+12,:]=xs[base:base+12,:].astype(BF)
        return 0
    lax.fori_loop(0,3,pair,0)

def prep_bias(position_bias):
    b=position_bias*np.float32(LOG2E)
    lvl=np.arange(WIN)//72; row=np.arange(WIN)//12%6
    outs=[]
    for le in range(2):
        for ve in range(2):
            g=2*le*(row>=3)+ve*lvl
            outs.append((g[:,None]!=g[None,:]).astype(np.float32)*np.float32(-1e30))
    return (b[None]+jnp.asarray(np.stack(outs))[:,None]).reshape(4,HEADS*WIN,WIN)

def compute(shifted, lat_edge, position_bias, g1, wqkv, wp, g2, wup, wdn):
    bias=prep_bias(position_bias)
    wq=jnp.pad(wqkv.reshape(D,3,D),((0,0),(0,0),(0,64))).reshape(D,768)
    full=lambda *s: pl.BlockSpec(s,lambda i:(0,)*len(s),pipeline_mode=pl.Buffered(1))
    return pl.pallas_call(
        kernel, grid=(12,),
        in_specs=[pl.BlockSpec(memory_space=pltpu.SMEM),
          pl.BlockSpec((6,6,24,D),lambda i:(0,i,0,0)),
          full(4,HEADS*WIN,WIN),full(1,D),full(D,768),full(D,D),full(1,D),full(D,768),full(D,768)],
        out_specs=pl.BlockSpec((6,6,24,D),lambda i:(0,i,0,0)),
        out_shape=jax.ShapeDtypeStruct((6,72,24,D),BF),
        scratch_shapes=[pltpu.VMEM((2*WIN,D),F32),pltpu.VMEM((2,HEADS*WIN,WIN),F32),pltpu.VMEM((2,HEADS*WIN,WIN),BF),pltpu.VMEM((2*WIN,256),BF)],
        compiler_params=pltpu.CompilerParams(vmem_limit_bytes=56<<20),
    )(lat_edge,shifted,bias,g1.reshape(1,D),wq,wp,g2.reshape(1,D),wup,wdn.T)


CAP = 32
DEV = 128
TN = (((0,), (0,)), ((), ()))
UN=8
def pack_kernel(tgt_ref, cell_ref, cnt_ref, val_ref, wt_ref, out_ref, pay, buf):
    n=val_ref.shape[0]
    eye=(lax.broadcasted_iota(jnp.int32,(8,64),0)==lax.broadcasted_iota(jnp.int32,(8,64),1)).astype(BF)
    for c in range(0,n,512):
        y=lax.dot_general(val_ref[c:c+512,:],wt_ref[...],NT,preferred_element_type=F32)
        pay[pl.ds(2*c,512,stride=2),:]=y[:,0:128]
        cell=cell_ref[0:1,c:c+512]
        ids=jnp.concatenate([(cell>>7).astype(F32),(cell&127).astype(F32),jnp.zeros((6,512),F32)],axis=0).astype(BF)
        mark=lax.dot_general(ids,eye,TN,preferred_element_type=F32)
        pay[pl.ds(2*c+1,512,stride=2),:]=jnp.concatenate([y[:,128:192],mark],axis=1)
    def zero(g,_):
        buf[pl.ds(pl.multiple_of(g*512,512),512),:]=jnp.zeros((512,128),F32)
        return 0
    lax.fori_loop(0,2*DEV*CAP//512,zero,0)
    count=cnt_ref[0]
    def body(g,_):
        for u in range(UN):
            i=g*UN+u
            buf[pl.ds(2*tgt_ref[i],2),:]=pay[pl.ds(2*i,2),:]
        return 0
    lax.fori_loop(0,(count+UN-1)//UN,body,0)
    def conv(g,_):
        r=pl.multiple_of(g*256,256)
        out_ref[pl.ds(r,256),0:128]=buf[pl.ds(2*r,256,stride=2),:].astype(BF)
        out_ref[pl.ds(r,256),128:256]=buf[pl.ds(2*r+1,256,stride=2),:].astype(BF)
        return 0
    lax.fori_loop(0,DEV*CAP//256,conv,0)

def pack(targets, cells, count, values, w_obs):
    n=values.shape[0]
    sm=pl.BlockSpec(memory_space=pltpu.SMEM); vm=pl.BlockSpec(memory_space=pltpu.VMEM)
    return pl.pallas_call(pack_kernel,in_specs=[sm,vm,sm,vm,vm],out_specs=vm,
        out_shape=jax.ShapeDtypeStruct((DEV*CAP,256),BF),
        scratch_shapes=[pltpu.VMEM((2*n,128),F32),pltpu.VMEM((2*DEV*CAP+16,128),F32)],
        compiler_params=pltpu.CompilerParams(vmem_limit_bytes=40<<20),
    )(targets,cells.reshape(1,n),count,values,w_obs.T)

NACC=3
SUN=8
def scatter_kernel(recv_ref, tok_ref, out_ref, rows, ids_v, ids_s, sem, *accs):
    cells=tok_ref.shape[0]
    sel=jnp.where(lax.broadcasted_iota(jnp.int32,(8,256),1)==192,128.0,jnp.where(lax.broadcasted_iota(jnp.int32,(8,256),1)==193,1.0,0.0)).astype(BF)
    n=recv_ref.shape[0]
    for c in range(0,n,512):
        ids=lax.dot_general(sel,recv_ref[c:c+512,:],NT,preferred_element_type=F32)
        ids_v[0:1,c:c+512]=(ids[0:1]+0.5).astype(jnp.int32)
    cp=pltpu.make_async_copy(ids_v,ids_s,sem)
    cp.start()
    def prep(g,_):
        r=pl.multiple_of(g*256,256)
        rows[pl.ds(2*r,256,stride=2),:]=recv_ref[pl.ds(r,256),0:128].astype(F32)
        rows[pl.ds(2*r+1,256,stride=2),:]=recv_ref[pl.ds(r,256),128:256].astype(F32)
        return 0
    lax.fori_loop(0,n//256,prep,0)
    def init(g,_):
        r=pl.multiple_of(g*144,144)
        t=tok_ref[pl.ds(r,144),:].astype(F32)
        accs[0][pl.ds(2*r,144,stride=2),:]=t[:,0:128]
        accs[0][pl.ds(2*r+1,144,stride=2),0:64]=t[:,128:192]
        for a in accs[1:]: a[pl.ds(2*r,288),:]=jnp.zeros((288,128),F32)
        return 0
    lax.fori_loop(0,cells//144,init,0)
    cp.wait()
    per=n//NACC
    def body(i,_):
        for a in range(NACC):
            j=a*per+i
            c=ids_s[0,j]
            accs[a][pl.ds(2*c,2),:]=accs[a][pl.ds(2*c,2),:]+rows[pl.ds(2*j,2),:]
        return 0
    lax.fori_loop(0,per,body,0,unroll=SUN)
    for j in range(per*NACC,n):
        c=ids_s[0,j]
        accs[0][pl.ds(2*c,2),:]=accs[0][pl.ds(2*c,2),:]+rows[pl.ds(2*j,2),:]
    def fin(g,_):
        r=pl.multiple_of(g*144,144)
        t=accs[0][pl.ds(2*r,144,stride=2),:]
        for a in accs[1:]: t=t+a[pl.ds(2*r,144,stride=2),:]
        out_ref[pl.ds(r,144),0:128]=t.astype(BF)
        t=accs[0][pl.ds(2*r+1,144,stride=2),:]
        for a in accs[1:]: t=t+a[pl.ds(2*r+1,144,stride=2),:]
        out_ref[pl.ds(r,144),128:192]=t[:,0:64].astype(BF)
        return 0
    lax.fori_loop(0,cells//144,fin,0)

def scatter(recv, tokens):
    cells=6*72*24
    tok=tokens.reshape(cells,D)
    vm=pl.BlockSpec(memory_space=pltpu.VMEM)
    n=recv.shape[0]
    out=pl.pallas_call(scatter_kernel,in_specs=[vm,vm],out_specs=vm,
        out_shape=jax.ShapeDtypeStruct((cells,D),BF),
        scratch_shapes=[pltpu.VMEM((2*n,128),F32),pltpu.VMEM((1,n),jnp.int32),pltpu.SMEM((1,n),jnp.int32),pltpu.SemaphoreType.DMA]+[pltpu.VMEM((2*cells,128),F32)]*NACC,
        compiler_params=pltpu.CompilerParams(vmem_limit_bytes=60<<20),
    )(recv,tok)
    return out.reshape(tokens.shape)


def passed_along(block, axis, distance):
    devices = range(lax.axis_size(axis))
    route = [((i - distance) % len(devices), i) for i in devices]
    return lax.ppermute(block, axis, route)


def on_device(
    tokens,
    obs_values,
    obs_dest,
    obs_cell,
    obs_count,
    w_obs,
    ln1_gain,
    w_qkv,
    position_bias,
    w_proj,
    ln2_gain,
    w_up,
    w_down,
):
    levels, lat_rows, lon_cols, features = tokens.shape
    lon_count = lax.axis_size("lon")
    lat_count = lax.axis_size("lat")
    devices = lon_count * lat_count
    row_count = obs_values.shape[0]
    capacity = 2 * row_count // devices
    position = jnp.arange(row_count, dtype=jnp.int32)
    is_live = position < obs_count[0]
    matches = (
        (obs_dest[:, None] == jnp.arange(devices, dtype=jnp.int32)[None, :]) & is_live[:, None]
    ).astype(jnp.int32)
    earlier = jnp.cumsum(matches, axis=0) - matches
    slot_ids = jnp.sum(earlier * matches, axis=1)
    targets = jnp.where(is_live, obs_dest * capacity + slot_ids, devices * capacity)
    buffer = pack(targets, obs_cell, obs_count, obs_values, w_obs)
    received = lax.all_to_all(
        buffer.reshape(devices, capacity, 256), ("lon", "lat"), split_axis=0, concat_axis=0, tiled=True
    )
    stream = scatter(received.reshape(devices * capacity, 256), tokens)
    half_lat = WLAT // 2
    half_lon = WLON // 2
    lat_index = lax.axis_index("lat")
    arrived = passed_along(stream[:, :, :half_lon], "lon", -1)
    widened = jnp.concatenate([stream[:, :, half_lon:], arrived], axis=2)
    arrived = passed_along(widened[:, :half_lat], "lat", -1)
    shifted = jnp.concatenate([widened[:, half_lat:], arrived], axis=1)
    edge = (lat_index == lat_count - 1).astype(jnp.int32).reshape(1)
    result = compute(
        shifted, edge, position_bias, ln1_gain, w_qkv, w_proj, ln2_gain, w_up, w_down
    )
    arrived = passed_along(result[:, lat_rows - half_lat :], "lat", 1)
    widened = jnp.concatenate([arrived, result[:, : lat_rows - half_lat]], axis=1)
    arrived = passed_along(widened[:, :, lon_cols - half_lon :], "lon", 1)
    return jnp.concatenate([arrived, widened[:, :, : lon_cols - half_lon]], axis=2)


def solution(mesh):
    in_specs = (
        P(None, "lat", "lon", None),
        P(("lon", "lat"), None),
        P(("lon", "lat")),
        P(("lon", "lat")),
        P(("lon", "lat")),
        P(),
        P(),
        P(),
        P(),
        P(),
        P(),
        P(),
        P(),
    )
    out_specs = P(None, "lat", "lon", None)
    return jax.shard_map(
        on_device, mesh=mesh, in_specs=in_specs, out_specs=out_specs, check_vma=False
    )
```

```python
import math

import jax
import jax.numpy as jnp
import numpy as np
from jax import lax
from jax.experimental import pallas as pl
from jax.experimental.pallas import tpu as pltpu
from jax.sharding import PartitionSpec as P

WZ = 2
WLAT = 6
WLON = 12
F32=jnp.float32; BF=jnp.bfloat16
WIN=144; D=192; HEADS=6; HD=32
NT=(((1,),(1,)),((),()))
LOG2E=math.log2(math.e)

def dot(a,b): return jnp.dot(a,b,preferred_element_type=F32)
def dot_nt(a,b): return lax.dot_general(a,b,NT,preferred_element_type=F32)

def norm(x, gain):
    mean=jnp.mean(x,axis=-1,keepdims=True)
    c=x-mean
    var=jnp.mean(c*c,axis=-1,keepdims=True)
    return (c*lax.rsqrt(var+1e-5)*gain).astype(BF)

def gelu(x):
    h=0.5*x
    return h+h*lax.erf(x*np.float32(math.sqrt(0.5)))

def head_mask(shape, h, width=HD):
    lane=lax.broadcasted_iota(jnp.int32,shape,len(shape)-1)
    return (lane>=h*width)&(lane<(h+1)*width)

GROUPS=((0,4,0),(4,2,128))
MESH=pl.DeviceIdType.MESH

def prep_bias(position_bias):
    b=position_bias*np.float32(LOG2E)
    lvl=np.arange(WIN)//72; row=np.arange(WIN)//12%6
    outs=[]
    for le in range(2):
        for ve in range(2):
            g=2*le*(row>=3)+ve*lvl
            outs.append((g[:,None]!=g[None,:]).astype(np.float32)*np.float32(-1e30))
    return (b[None]+jnp.asarray(np.stack(outs))[:,None]).reshape(4,HEADS*WIN,WIN)


CAP = 32
DEV = 128
TN = (((0,), (0,)), ((), ()))
UN=8
def pack_kernel(tgt_ref, cell_ref, cnt_ref, val_ref, wt_ref, out_ref, pay, buf):
    n=val_ref.shape[0]
    eye=(lax.broadcasted_iota(jnp.int32,(8,64),0)==lax.broadcasted_iota(jnp.int32,(8,64),1)).astype(BF)
    for c in range(0,n,512):
        y=lax.dot_general(val_ref[c:c+512,:],wt_ref[...],NT,preferred_element_type=F32)
        pay[pl.ds(2*c,512,stride=2),:]=y[:,0:128]
        cell=cell_ref[0:1,c:c+512]
        ids=jnp.concatenate([(cell>>7).astype(F32),(cell&127).astype(F32),jnp.zeros((6,512),F32)],axis=0).astype(BF)
        mark=lax.dot_general(ids,eye,TN,preferred_element_type=F32)
        pay[pl.ds(2*c+1,512,stride=2),:]=jnp.concatenate([y[:,128:192],mark],axis=1)
    def zero(g,_):
        buf[pl.ds(pl.multiple_of(g*512,512),512),:]=jnp.zeros((512,128),F32)
        return 0
    lax.fori_loop(0,2*DEV*CAP//512,zero,0)
    count=cnt_ref[0]
    def body(g,_):
        for u in range(UN):
            i=g*UN+u
            buf[pl.ds(2*tgt_ref[i],2),:]=pay[pl.ds(2*i,2),:]
        return 0
    lax.fori_loop(0,(count+UN-1)//UN,body,0)
    def conv(g,_):
        r=pl.multiple_of(g*256,256)
        out_ref[pl.ds(r,256),0:128]=buf[pl.ds(2*r,256,stride=2),:].astype(BF)
        out_ref[pl.ds(r,256),128:256]=buf[pl.ds(2*r+1,256,stride=2),:].astype(BF)
        return 0
    lax.fori_loop(0,DEV*CAP//256,conv,0)

def pack(targets, cells, count, values, w_obs):
    n=values.shape[0]
    sm=pl.BlockSpec(memory_space=pltpu.SMEM); vm=pl.BlockSpec(memory_space=pltpu.VMEM)
    return pl.pallas_call(pack_kernel,in_specs=[sm,vm,sm,vm,vm],out_specs=vm,
        out_shape=jax.ShapeDtypeStruct((DEV*CAP,256),BF),
        scratch_shapes=[pltpu.VMEM((2*n,128),F32),pltpu.VMEM((2*DEV*CAP+16,128),F32)],
        compiler_params=pltpu.CompilerParams(vmem_limit_bytes=40<<20),
    )(targets,cells.reshape(1,n),count,values,w_obs.T)

NACC=3
SUN=8
def scatter_kernel(recv_ref, tok_ref, out_ref, rows, ids_v, ids_s, sem, *accs):
    cells=tok_ref.shape[0]
    sel=jnp.where(lax.broadcasted_iota(jnp.int32,(8,256),1)==192,128.0,jnp.where(lax.broadcasted_iota(jnp.int32,(8,256),1)==193,1.0,0.0)).astype(BF)
    n=recv_ref.shape[0]
    for c in range(0,n,512):
        ids=lax.dot_general(sel,recv_ref[c:c+512,:],NT,preferred_element_type=F32)
        ids_v[0:1,c:c+512]=(ids[0:1]+0.5).astype(jnp.int32)
    cp=pltpu.make_async_copy(ids_v,ids_s,sem)
    cp.start()
    def prep(g,_):
        r=pl.multiple_of(g*256,256)
        rows[pl.ds(2*r,256,stride=2),:]=recv_ref[pl.ds(r,256),0:128].astype(F32)
        rows[pl.ds(2*r+1,256,stride=2),:]=recv_ref[pl.ds(r,256),128:256].astype(F32)
        return 0
    lax.fori_loop(0,n//256,prep,0)
    def init(g,_):
        r=pl.multiple_of(g*144,144)
        t=tok_ref[pl.ds(r,144),:].astype(F32)
        accs[0][pl.ds(2*r,144,stride=2),:]=t[:,0:128]
        accs[0][pl.ds(2*r+1,144,stride=2),0:64]=t[:,128:192]
        for a in accs[1:]: a[pl.ds(2*r,288),:]=jnp.zeros((288,128),F32)
        return 0
    lax.fori_loop(0,cells//144,init,0)
    cp.wait()
    per=n//NACC
    def body(i,_):
        for a in range(NACC):
            j=a*per+i
            c=ids_s[0,j]
            accs[a][pl.ds(2*c,2),:]=accs[a][pl.ds(2*c,2),:]+rows[pl.ds(2*j,2),:]
        return 0
    lax.fori_loop(0,per,body,0,unroll=SUN)
    for j in range(per*NACC,n):
        c=ids_s[0,j]
        accs[0][pl.ds(2*c,2),:]=accs[0][pl.ds(2*c,2),:]+rows[pl.ds(2*j,2),:]
    def fin(g,_):
        r=pl.multiple_of(g*144,144)
        t=accs[0][pl.ds(2*r,144,stride=2),:]
        for a in accs[1:]: t=t+a[pl.ds(2*r,144,stride=2),:]
        out_ref[pl.ds(r,144),0:128]=t.astype(BF)
        t=accs[0][pl.ds(2*r+1,144,stride=2),:]
        for a in accs[1:]: t=t+a[pl.ds(2*r+1,144,stride=2),:]
        out_ref[pl.ds(r,144),128:192]=t[:,0:64].astype(BF)
        return 0
    lax.fori_loop(0,cells//144,fin,0)

def scatter(recv, tokens):
    cells=6*72*24
    tok=tokens.reshape(cells,D)
    vm=pl.BlockSpec(memory_space=pltpu.VMEM)
    n=recv.shape[0]
    out=pl.pallas_call(scatter_kernel,in_specs=[vm,vm],out_specs=vm,
        out_shape=jax.ShapeDtypeStruct((cells,D),BF),
        scratch_shapes=[pltpu.VMEM((2*n,128),F32),pltpu.VMEM((1,n),jnp.int32),pltpu.SMEM((1,n),jnp.int32),pltpu.SemaphoreType.DMA]+[pltpu.VMEM((2*cells,128),F32)]*NACC,
        compiler_params=pltpu.CompilerParams(vmem_limit_bytes=60<<20),
    )(recv,tok)
    return out.reshape(tokens.shape)


def attend(xs, s_ref, p_ref, ctx_ref, bias_ref, var, g1_ref, wqkv_ref, wp_ref, g2_ref, wup_ref, wdnt_ref):
    zero = jnp.zeros((), BF)
    n1 = norm(xs[...], g1_ref[...])
    q_all = (dot(n1, wqkv_ref[:, 0:256]) * np.float32(LOG2E / math.sqrt(HD))).astype(BF)
    k_all = dot(n1, wqkv_ref[:, 256:512]).astype(BF)
    v_all = dot(n1, wqkv_ref[:, 512:768]).astype(BF)
    for w in range(2):
        sl = slice(w * WIN, (w + 1) * WIN)
        for h0, nh, l0 in GROUPS:
            qg = q_all[sl, l0 : l0 + 128]
            kg = k_all[sl, l0 : l0 + 128]
            qs = jnp.concatenate(
                [jnp.where(head_mask((WIN, 128), h), qg, zero) for h in range(nh)], axis=0
            )
            s_ref[w, h0 * WIN : (h0 + nh) * WIN, :] = dot_nt(qs, kg)
    for w in range(2):
        sl = slice(w * WIN, (w + 1) * WIN)
        sums = []
        for h in range(HEADS):
            rows = slice(h * WIN, (h + 1) * WIN)
            s = s_ref[w, rows, :] + bias_ref[var[w], rows, :]
            p = jnp.exp2(s - jnp.max(s, axis=-1, keepdims=True))
            sums.append(jnp.sum(p, axis=-1, keepdims=True))
            p_ref[w, rows, :] = p.astype(BF)
        for h0, nh, l0 in GROUPS:
            o = dot(p_ref[w, h0 * WIN : (h0 + nh) * WIN, :], v_all[sl, l0 : l0 + 128])
            c = o[:WIN]
            total = sums[h0] * jnp.ones((1, 128), F32)
            for h in range(1, nh):
                mask = head_mask((WIN, 128), h)
                c = jnp.where(mask, o[h * WIN : (h + 1) * WIN], c)
                total = jnp.where(mask, sums[h0 + h], total)
            ctx_ref[sl, l0 : l0 + 128] = (c * (1.0 / total)).astype(BF)
    att = (xs[...] + dot(ctx_ref[:, :D], wp_ref[...])).astype(BF).astype(F32)
    n2 = norm(att, g2_ref[...])
    acc = att
    for j in range(3):
        hid = gelu(dot(n2, wup_ref[:, j * 256 : (j + 1) * 256])).astype(BF)
        acc = acc + dot_nt(hid, wdnt_ref[:, j * 256 : (j + 1) * 256])
    xs[...] = acc


def block_kernel(
    x_hbm, bias_ref, g1_ref, wqkv_ref, wp_ref, g2_ref, wup_ref, wdnt_ref, o_ref,
    xe, from_right, from_left, to_right, to_left, back_left, back_right, back_lat, back_diag,
    xs, s_ref, p_ref, ctx_ref, send_sem, recv_sem, local_sem,
):
    lon = lax.axis_index("lon")
    lat = lax.axis_index("lat")
    n_lon = lax.axis_size("lon")
    n_lat = lax.axis_size("lat")
    east = lax.rem(lon + 1, n_lon)
    west = lax.rem(lon + n_lon - 1, n_lon)
    north = lax.rem(lat + 1, n_lat)
    south = lax.rem(lat + n_lat - 1, n_lat)

    locals_ = [
        pltpu.make_async_copy(
            x_hbm.at[:, r0:r1], xe.at[:, r0:r1], local_sem.at[n]
        )
        for n, (r0, r1) in enumerate(((0, 39), (39, 72)))
    ]
    for copy in locals_:
        copy.start()

    barrier = pltpu.get_barrier_semaphore()
    partners = ((east, lat), (west, lat), (lon, north), (lon, south), (east, south), (west, north))
    for partner in partners:
        pl.semaphore_signal(barrier, inc=1, device_id=partner, device_id_type=MESH)
    pl.semaphore_wait(barrier, len(partners))

    def remote(n, src, dst, target):
        return pltpu.make_async_remote_copy(
            src_ref=src, dst_ref=dst, send_sem=send_sem.at[n], recv_sem=recv_sem.at[n],
            device_id=target, device_id_type=MESH,
        )

    halo = [
        remote(0, x_hbm.at[:, 3:39, 0:8], from_right, (west, lat)),
        remote(1, x_hbm.at[:, 39:72, 16:24], from_left.at[:, 0:33], (east, lat)),
        remote(2, x_hbm.at[:, 0:3], xe.at[:, 72:75], (lon, south)),
        remote(3, x_hbm.at[:, 0:3, 16:24], from_left.at[:, 33:36], (east, south)),
    ]
    home_east = [
        remote(4 + j, to_right.at[:, 12 * j : 12 * j + 12], back_left.at[:, 12 * j : 12 * j + 12], (east, lat))
        for j in range(3)
    ]
    home_west = [
        remote(7 + j, to_left.at[:, 12 * j : end], back_right.at[:, 12 * j : end], (west, lat))
        for j, end in enumerate((12, 24, 33))
    ]
    home_diag = remote(10, to_left.at[:, 33:36], back_diag, (west, north))
    home_lat = remote(11, o_ref.at[:, 72:75], back_lat, (lon, north))
    for copy in halo:
        copy.start()
    locals_[0].wait()

    def step(s, _):
        phase = s // 9
        turn = lax.rem(s, 9) // 3
        k = lax.rem(s, 3)
        j = jnp.where(phase < 2, turn, 5 - turn)
        levels = (2 * k + 1, lax.rem(2 * k + 2, 6))
        inner = (phase == 0) | (phase == 3)

        @pl.when(s == 9)
        def _():
            halo[0].wait_recv()

        @pl.when(s == 18)
        def _():
            locals_[1].wait()
            for copy in halo[1:]:
                copy.wait_recv()

        def places():
            for i in range(2):
                for w in range(2):
                    for r in range(6):
                        yield levels[i], 3 + 6 * (2 * j + w) + r, w * WIN + (i * 6 + r) * 12

        @pl.when(inner)
        def _():
            for level, row, at in places():
                xs[at : at + 12, :] = xe[level, row].astype(F32)[6:18]

        @pl.when(phase == 1)
        def _():
            for level, row, at in places():
                xs[at : at + 6, :] = xe[level, row, 16:24].astype(F32)[2:8]
                xs[at + 6 : at + 12, :] = from_right[level, row - 3].astype(F32)[0:6]

        @pl.when(phase == 2)
        def _():
            for level, row, at in places():
                xs[at : at + 6, :] = from_left[level, row - 39].astype(F32)[2:8]
                xs[at + 6 : at + 12, :] = xe[level, row, 0:8].astype(F32)[0:6]

        lat_edge = ((j == 5) & (lat == n_lat - 1)).astype(jnp.int32)
        level_edge = (k == 2).astype(jnp.int32)
        attend(
            xs, s_ref, p_ref, ctx_ref, bias_ref, (level_edge, 2 * lat_edge + level_edge),
            g1_ref, wqkv_ref, wp_ref, g2_ref, wup_ref, wdnt_ref,
        )

        @pl.when(inner)
        def _():
            for level, row, at in places():
                o_ref[level, row, 6:18, :] = xs[at : at + 12, :].astype(BF)

        @pl.when(phase == 1)
        def _():
            for level, row, at in places():
                o_ref[level, row, 18:24, :] = xs[at : at + 6, :].astype(BF)
                to_right[level, row - 3, 0:6, :] = xs[at + 6 : at + 12, :].astype(BF)

        @pl.when(phase == 2)
        def _():
            for level, row, at in places():
                to_left[level, row - 39, 2:8, :] = xs[at : at + 6, :].astype(BF)
                o_ref[level, row, 0:6, :] = xs[at + 6 : at + 12, :].astype(BF)

        for n in range(3):
            @pl.when(s == 11 + 3 * n)
            def _(n=n):
                home_east[n].start()

            @pl.when(s == 20 + 3 * n)
            def _(n=n):
                home_west[2 - n].start()
                if n == 0:
                    home_diag.start()

        @pl.when(s == 29)
        def _():
            home_lat.start()

        return 0

    lax.fori_loop(0, 36, step, 0)
    for copy in home_east:
        copy.wait_recv()
    home_lat.wait_recv()
    home_diag.wait_recv()
    for copy in home_west:
        copy.wait_recv()

    def merge(level, _):
        for r in range(36):
            o_ref[level, 3 + r, 0:6, :] = back_left[level, r, 0:6, :]
        for r in range(33):
            o_ref[level, 39 + r, 18:24, :] = back_right[level, r, 2:8, :]
        for r in range(3):
            o_ref[level, r, 0:18, :] = back_lat[level, r, 0:18, :]
            o_ref[level, r, 18:24, :] = back_diag[level, r, 2:8, :]
        return 0

    lax.fori_loop(0, 6, merge, 0)
    for copy in (*halo, *home_east, *home_west, home_diag, home_lat):
        copy.wait_send()


def block(stream, position_bias, g1, wqkv, wp, g2, wup, wdn):
    bias = prep_bias(position_bias)
    wq = jnp.pad(wqkv.reshape(D, 3, D), ((0, 0), (0, 0), (0, 64))).reshape(D, 768)
    vm = pl.BlockSpec(memory_space=pltpu.VMEM)
    slab = pltpu.VMEM((6, 36, 8, D), BF)
    out = pl.pallas_call(
        block_kernel,
        in_specs=[pl.BlockSpec(memory_space=pl.ANY)] + [vm] * 7,
        out_specs=vm,
        out_shape=jax.ShapeDtypeStruct((6, 75, 24, D), BF),
        scratch_shapes=[
            pltpu.VMEM((6, 75, 24, D), BF),
            slab, slab, slab, slab,
            slab, pltpu.VMEM((6, 33, 8, D), BF),
            pltpu.VMEM((6, 3, 24, D), BF), pltpu.VMEM((6, 3, 8, D), BF),
            pltpu.VMEM((2 * WIN, D), F32),
            pltpu.VMEM((2, HEADS * WIN, WIN), F32),
            pltpu.VMEM((2, HEADS * WIN, WIN), BF),
            pltpu.VMEM((2 * WIN, 256), BF),
            pltpu.SemaphoreType.DMA((12,)),
            pltpu.SemaphoreType.DMA((12,)),
            pltpu.SemaphoreType.DMA((2,)),
        ],
        compiler_params=pltpu.CompilerParams(
            collective_id=0, has_side_effects=True, vmem_limit_bytes=56 << 20
        ),
    )(stream, bias, g1.reshape(1, D), wq, wp, g2.reshape(1, D), wup, wdn.T)
    return out[:, :72]


def on_device(
    tokens,
    obs_values,
    obs_dest,
    obs_cell,
    obs_count,
    w_obs,
    ln1_gain,
    w_qkv,
    position_bias,
    w_proj,
    ln2_gain,
    w_up,
    w_down,
):
    levels, lat_rows, lon_cols, features = tokens.shape
    lon_count = lax.axis_size("lon")
    lat_count = lax.axis_size("lat")
    devices = lon_count * lat_count
    row_count = obs_values.shape[0]
    capacity = 2 * row_count // devices
    position = jnp.arange(row_count, dtype=jnp.int32)
    is_live = position < obs_count[0]
    matches = (
        (obs_dest[:, None] == jnp.arange(devices, dtype=jnp.int32)[None, :]) & is_live[:, None]
    ).astype(jnp.int32)
    earlier = jnp.cumsum(matches, axis=0) - matches
    slot_ids = jnp.sum(earlier * matches, axis=1)
    targets = jnp.where(is_live, obs_dest * capacity + slot_ids, devices * capacity)
    buffer = pack(targets, obs_cell, obs_count, obs_values, w_obs)
    received = lax.all_to_all(
        buffer.reshape(devices, capacity, 256), ("lon", "lat"), split_axis=0, concat_axis=0, tiled=True
    )
    stream = scatter(received.reshape(devices * capacity, 256), tokens)
    return block(stream, position_bias, ln1_gain, w_qkv, w_proj, ln2_gain, w_up, w_down)


def solution(mesh):
    in_specs = (
        P(None, "lat", "lon", None),
        P(("lon", "lat"), None),
        P(("lon", "lat")),
        P(("lon", "lat")),
        P(("lon", "lat")),
        P(),
        P(),
        P(),
        P(),
        P(),
        P(),
        P(),
        P(),
    )
    out_specs = P(None, "lat", "lon", None)
    return jax.shard_map(
        on_device, mesh=mesh, in_specs=in_specs, out_specs=out_specs, check_vma=False
    )
```

```python
import math

import jax
import jax.numpy as jnp
import numpy as np
from jax import lax
from jax.experimental import pallas as pl
from jax.experimental.pallas import tpu as pltpu
from jax.sharding import PartitionSpec as P

WZ = 2
WLAT = 6
WLON = 12
F32=jnp.float32; BF=jnp.bfloat16
WIN=144; D=192; HEADS=6; HD=32
NT=(((1,),(1,)),((),()))
LOG2E=math.log2(math.e)

def dot(a,b): return jnp.dot(a,b,preferred_element_type=F32)
def dot_nt(a,b): return lax.dot_general(a,b,NT,preferred_element_type=F32)

def norm(x, gain):
    mean=jnp.mean(x,axis=-1,keepdims=True)
    c=x-mean
    var=jnp.mean(c*c,axis=-1,keepdims=True)
    return (c*lax.rsqrt(var+1e-5)*gain).astype(BF)

def gelu(x):
    h=0.5*x
    return h+h*lax.erf(x*np.float32(math.sqrt(0.5)))

def head_mask(shape, h, width=HD):
    lane=lax.broadcasted_iota(jnp.int32,shape,len(shape)-1)
    return (lane>=h*width)&(lane<(h+1)*width)

GROUPS=((0,4,0),(4,2,128))
MESH=pl.DeviceIdType.MESH

def prep_bias(position_bias):
    b=position_bias*np.float32(LOG2E)
    lvl=np.arange(WIN)//72; row=np.arange(WIN)//12%6
    outs=[]
    for le in range(2):
        for ve in range(2):
            g=2*le*(row>=3)+ve*lvl
            outs.append((g[:,None]!=g[None,:]).astype(np.float32)*np.float32(-1e30))
    return (b[None]+jnp.asarray(np.stack(outs))[:,None]).reshape(4,HEADS*WIN,WIN)


CAP = 32
DEV = 128
TN = (((0,), (0,)), ((), ()))
UN=8
def pack_kernel(tgt_ref, cell_ref, cnt_ref, val_ref, wt_ref, out_ref, pay, buf):
    n=val_ref.shape[0]
    eye=(lax.broadcasted_iota(jnp.int32,(8,64),0)==lax.broadcasted_iota(jnp.int32,(8,64),1)).astype(BF)
    for c in range(0,n,512):
        y=lax.dot_general(val_ref[c:c+512,:],wt_ref[...],NT,preferred_element_type=F32)
        pay[pl.ds(2*c,512,stride=2),:]=y[:,0:128]
        cell=cell_ref[0:1,c:c+512]
        ids=jnp.concatenate([(cell>>7).astype(F32),(cell&127).astype(F32),jnp.zeros((6,512),F32)],axis=0).astype(BF)
        mark=lax.dot_general(ids,eye,TN,preferred_element_type=F32)
        pay[pl.ds(2*c+1,512,stride=2),:]=jnp.concatenate([y[:,128:192],mark],axis=1)
    def zero(g,_):
        buf[pl.ds(pl.multiple_of(g*512,512),512),:]=jnp.zeros((512,128),F32)
        return 0
    lax.fori_loop(0,2*DEV*CAP//512,zero,0)
    count=cnt_ref[0]
    def body(g,_):
        for u in range(UN):
            i=g*UN+u
            buf[pl.ds(2*tgt_ref[i],2),:]=pay[pl.ds(2*i,2),:]
        return 0
    lax.fori_loop(0,(count+UN-1)//UN,body,0)
    def conv(g,_):
        r=pl.multiple_of(g*256,256)
        out_ref[pl.ds(r,256),0:128]=buf[pl.ds(2*r,256,stride=2),:].astype(BF)
        out_ref[pl.ds(r,256),128:256]=buf[pl.ds(2*r+1,256,stride=2),:].astype(BF)
        return 0
    lax.fori_loop(0,DEV*CAP//256,conv,0)

def pack(targets, cells, count, values, w_obs):
    n=values.shape[0]
    sm=pl.BlockSpec(memory_space=pltpu.SMEM); vm=pl.BlockSpec(memory_space=pltpu.VMEM)
    return pl.pallas_call(pack_kernel,in_specs=[sm,vm,sm,vm,vm],out_specs=vm,
        out_shape=jax.ShapeDtypeStruct((DEV*CAP,256),BF),
        scratch_shapes=[pltpu.VMEM((2*n,128),F32),pltpu.VMEM((2*DEV*CAP+16,128),F32)],
        compiler_params=pltpu.CompilerParams(vmem_limit_bytes=16<<20),
    )(targets,cells.reshape(1,n),count,values,w_obs.T)

NACC=2
SUN=8
def scatter_kernel(recv_ref, tok_ref, out_ref, rows, ids_v, ids_s, sem, *accs):
    cells=tok_ref.shape[0]
    sel=jnp.where(lax.broadcasted_iota(jnp.int32,(8,256),1)==192,128.0,jnp.where(lax.broadcasted_iota(jnp.int32,(8,256),1)==193,1.0,0.0)).astype(BF)
    n=recv_ref.shape[0]
    for c in range(0,n,512):
        ids=lax.dot_general(sel,recv_ref[c:c+512,:],NT,preferred_element_type=F32)
        ids_v[0:1,c:c+512]=(ids[0:1]+0.5).astype(jnp.int32)
    cp=pltpu.make_async_copy(ids_v,ids_s,sem)
    cp.start()
    def prep(g,_):
        r=pl.multiple_of(g*256,256)
        rows[pl.ds(2*r,256,stride=2),:]=recv_ref[pl.ds(r,256),0:128].astype(F32)
        rows[pl.ds(2*r+1,256,stride=2),:]=recv_ref[pl.ds(r,256),128:256].astype(F32)
        return 0
    lax.fori_loop(0,n//256,prep,0)
    def init(g,_):
        r=pl.multiple_of(g*144,144)
        t=tok_ref[pl.ds(r,144),:].astype(F32)
        accs[0][pl.ds(2*r,144,stride=2),:]=t[:,0:128]
        accs[0][pl.ds(2*r+1,144,stride=2),0:64]=t[:,128:192]
        for a in accs[1:]: a[pl.ds(2*r,288),:]=jnp.zeros((288,128),F32)
        return 0
    lax.fori_loop(0,cells//144,init,0)
    cp.wait()
    per=n//NACC
    def body(i,_):
        for a in range(NACC):
            j=a*per+i
            c=ids_s[0,j]
            accs[a][pl.ds(2*c,2),:]=accs[a][pl.ds(2*c,2),:]+rows[pl.ds(2*j,2),:]
        return 0
    lax.fori_loop(0,per,body,0,unroll=SUN)
    for j in range(per*NACC,n):
        c=ids_s[0,j]
        accs[0][pl.ds(2*c,2),:]=accs[0][pl.ds(2*c,2),:]+rows[pl.ds(2*j,2),:]
    def fin(g,_):
        r=pl.multiple_of(g*144,144)
        t=accs[0][pl.ds(2*r,144,stride=2),:]
        for a in accs[1:]: t=t+a[pl.ds(2*r,144,stride=2),:]
        out_ref[pl.ds(r,144),0:128]=t.astype(BF)
        t=accs[0][pl.ds(2*r+1,144,stride=2),:]
        for a in accs[1:]: t=t+a[pl.ds(2*r+1,144,stride=2),:]
        out_ref[pl.ds(r,144),128:192]=t[:,0:64].astype(BF)
        return 0
    lax.fori_loop(0,cells//144,fin,0)

def scatter(recv, tokens):
    cells=6*72*24
    tok=tokens.reshape(cells,D)
    vm=pl.BlockSpec(memory_space=pltpu.VMEM)
    n=recv.shape[0]
    out=pl.pallas_call(scatter_kernel,in_specs=[vm,vm],out_specs=vm,
        out_shape=jax.ShapeDtypeStruct((cells,D),BF),
        scratch_shapes=[pltpu.VMEM((2*n,128),F32),pltpu.VMEM((1,n),jnp.int32),pltpu.SMEM((1,n),jnp.int32),pltpu.SemaphoreType.DMA]+[pltpu.VMEM((2*cells,128),F32)]*NACC,
        compiler_params=pltpu.CompilerParams(vmem_limit_bytes=30<<20),
    )(recv,tok)
    return out.reshape(tokens.shape)


def attend(xs, qkv_ref, s_ref, p_ref, ctx_ref, bias_ref, variants, g1_ref, wqkv_ref, wp_ref, g2_ref, wup_ref, wdnt_ref):
    zero = jnp.zeros((), BF)
    count = len(variants)
    n1 = norm(xs[...], g1_ref[...])
    qkv_ref[:, 0:256] = (
        dot(n1, wqkv_ref[:, 0:256]) * np.float32(LOG2E / math.sqrt(HD))
    ).astype(BF)
    qkv_ref[:, 256:512] = dot(n1, wqkv_ref[:, 256:512]).astype(BF)
    qkv_ref[:, 512:768] = dot(n1, wqkv_ref[:, 512:768]).astype(BF)

    def scores(w):
        sl = slice(w * WIN, (w + 1) * WIN)
        for h0, nh, l0 in GROUPS:
            qg = qkv_ref[sl, l0 : l0 + 128]
            kg = qkv_ref[sl, 256 + l0 : 384 + l0]
            qs = jnp.concatenate(
                [jnp.where(head_mask((WIN, 128), h), qg, zero) for h in range(nh)], axis=0
            )
            s_ref[w % 2, h0 * WIN : (h0 + nh) * WIN, :] = dot_nt(qs, kg)

    def softmax(w):
        sl = slice(w * WIN, (w + 1) * WIN)
        sums = []
        for h in range(HEADS):
            rows = slice(h * WIN, (h + 1) * WIN)
            s = s_ref[w % 2, rows, :] + bias_ref[variants[w], rows, :]
            p = jnp.exp2(s - jnp.max(s, axis=-1, keepdims=True))
            sums.append(jnp.sum(p, axis=-1, keepdims=True))
            p_ref[w % 2, rows, :] = p.astype(BF)
        for h0, nh, l0 in GROUPS:
            o = dot(p_ref[w % 2, h0 * WIN : (h0 + nh) * WIN, :], qkv_ref[sl, 512 + l0 : 640 + l0])
            c = o[:WIN]
            total = sums[h0] * jnp.ones((1, 128), F32)
            for h in range(1, nh):
                mask = head_mask((WIN, 128), h)
                c = jnp.where(mask, o[h * WIN : (h + 1) * WIN], c)
                total = jnp.where(mask, sums[h0 + h], total)
            ctx_ref[sl, l0 : l0 + 128] = (c * (1.0 / total)).astype(BF)

    scores(0)
    for w in range(count):
        if w + 1 < count:
            scores(w + 1)
        softmax(w)
    att = (xs[...] + dot(ctx_ref[:, :D], wp_ref[...])).astype(BF).astype(F32)
    n2 = norm(att, g2_ref[...])
    acc = att
    for j in range(3):
        hid = gelu(dot(n2, wup_ref[:, j * 256 : (j + 1) * 256])).astype(BF)
        acc = acc + dot_nt(hid, wdnt_ref[:, j * 256 : (j + 1) * 256])
    xs[...] = acc


def block_kernel(
    x_hbm, bias_ref, g1_ref, wqkv_ref, wp_ref, g2_ref, wup_ref, wdnt_ref, o_ref,
    xe, from_right, from_left, to_right, to_left, back_left, back_right, back_lat, back_diag,
    xs, qkv_ref, s_ref, p_ref, ctx_ref, send_sem, recv_sem, local_sem,
):
    lon = lax.axis_index("lon")
    lat = lax.axis_index("lat")
    n_lon = lax.axis_size("lon")
    n_lat = lax.axis_size("lat")
    east = lax.rem(lon + 1, n_lon)
    west = lax.rem(lon + n_lon - 1, n_lon)
    north = lax.rem(lat + 1, n_lat)
    south = lax.rem(lat + n_lat - 1, n_lat)

    locals_ = [
        pltpu.make_async_copy(
            x_hbm.at[:, r0:r1], xe.at[:, r0:r1], local_sem.at[n]
        )
        for n, (r0, r1) in enumerate(((0, 39), (39, 72)))
    ]
    for copy in locals_:
        copy.start()

    barrier = pltpu.get_barrier_semaphore()
    partners = ((east, lat), (west, lat), (lon, north), (lon, south), (east, south), (west, north))
    for partner in partners:
        pl.semaphore_signal(barrier, inc=1, device_id=partner, device_id_type=MESH)
    pl.semaphore_wait(barrier, len(partners))

    def remote(n, src, dst, target):
        return pltpu.make_async_remote_copy(
            src_ref=src, dst_ref=dst, send_sem=send_sem.at[n], recv_sem=recv_sem.at[n],
            device_id=target, device_id_type=MESH,
        )

    halo = [
        remote(0, x_hbm.at[:, 3:39, 0:8], from_right, (west, lat)),
        remote(1, x_hbm.at[:, 39:72, 16:24], from_left.at[:, 0:33], (east, lat)),
        remote(2, x_hbm.at[:, 0:3], xe.at[:, 72:75], (lon, south)),
        remote(3, x_hbm.at[:, 0:3, 16:24], from_left.at[:, 33:36], (east, south)),
    ]
    home_east = [
        remote(4 + j, to_right.at[:, 12 * j : 12 * j + 12], back_left.at[:, 12 * j : 12 * j + 12], (east, lat))
        for j in range(3)
    ]
    home_west = [
        remote(7 + j, to_left.at[:, 12 * j : end], back_right.at[:, 12 * j : end], (west, lat))
        for j, end in enumerate((12, 24, 33))
    ]
    home_diag = remote(10, to_left.at[:, 33:36], back_diag, (west, north))
    home_lat = remote(11, o_ref.at[:, 72:75], back_lat, (lon, north))
    for copy in halo:
        copy.start()
    locals_[0].wait()

    def step(s, _):
        phase = s // 3
        turn = lax.rem(s, 3)
        j = jnp.where(phase < 2, turn, 5 - turn)
        inner = (phase == 0) | (phase == 3)

        @pl.when(s == 3)
        def _():
            halo[0].wait_recv()

        @pl.when(s == 6)
        def _():
            locals_[1].wait()
            for copy in halo[1:]:
                copy.wait_recv()

        def places():
            for w in range(6):
                for i in range(2):
                    for r in range(6):
                        level = (w // 2 * 2 + 1 + i) % 6
                        yield level, 3 + 6 * (2 * j + w % 2) + r, w * WIN + (i * 6 + r) * 12

        @pl.when(inner)
        def _():
            for level, row, at in places():
                xs[at : at + 12, :] = xe[level, row].astype(F32)[6:18]

        @pl.when(phase == 1)
        def _():
            for level, row, at in places():
                xs[at : at + 6, :] = xe[level, row, 16:24].astype(F32)[2:8]
                xs[at + 6 : at + 12, :] = from_right[level, row - 3].astype(F32)[0:6]

        @pl.when(phase == 2)
        def _():
            for level, row, at in places():
                xs[at : at + 6, :] = from_left[level, row - 39].astype(F32)[2:8]
                xs[at + 6 : at + 12, :] = xe[level, row, 0:8].astype(F32)[0:6]

        lat_edge = ((j == 5) & (lat == n_lat - 1)).astype(jnp.int32)
        variants = [w // 4 + (2 * lat_edge if w % 2 else 0) for w in range(6)]
        attend(
            xs, qkv_ref, s_ref, p_ref, ctx_ref, bias_ref, variants,
            g1_ref, wqkv_ref, wp_ref, g2_ref, wup_ref, wdnt_ref,
        )

        @pl.when(inner)
        def _():
            for level, row, at in places():
                o_ref[level, row, 6:18, :] = xs[at : at + 12, :].astype(BF)

        @pl.when(phase == 1)
        def _():
            for level, row, at in places():
                o_ref[level, row, 18:24, :] = xs[at : at + 6, :].astype(BF)
                to_right[level, row - 3, 0:6, :] = xs[at + 6 : at + 12, :].astype(BF)

        @pl.when(phase == 2)
        def _():
            for level, row, at in places():
                to_left[level, row - 39, 2:8, :] = xs[at : at + 6, :].astype(BF)
                o_ref[level, row, 0:6, :] = xs[at + 6 : at + 12, :].astype(BF)

        for n in range(3):
            @pl.when(s == 3 + n)
            def _(n=n):
                home_east[n].start()

            @pl.when(s == 6 + n)
            def _(n=n):
                home_west[2 - n].start()
                if n == 0:
                    home_diag.start()

        @pl.when(s == 9)
        def _():
            home_lat.start()

        return 0

    lax.fori_loop(0, 12, step, 0)
    for copy in home_east:
        copy.wait_recv()
    home_lat.wait_recv()
    home_diag.wait_recv()
    for copy in home_west:
        copy.wait_recv()

    def merge(level, _):
        for r in range(36):
            o_ref[level, 3 + r, 0:6, :] = back_left[level, r, 0:6, :]
        for r in range(33):
            o_ref[level, 39 + r, 18:24, :] = back_right[level, r, 2:8, :]
        for r in range(3):
            o_ref[level, r, 0:18, :] = back_lat[level, r, 0:18, :]
            o_ref[level, r, 18:24, :] = back_diag[level, r, 2:8, :]
        return 0

    lax.fori_loop(0, 6, merge, 0)
    for copy in (*halo, *home_east, *home_west, home_diag, home_lat):
        copy.wait_send()


def block(stream, position_bias, g1, wqkv, wp, g2, wup, wdn):
    bias = prep_bias(position_bias)
    wq = jnp.pad(wqkv.reshape(D, 3, D), ((0, 0), (0, 0), (0, 64))).reshape(D, 768)
    vm = pl.BlockSpec(memory_space=pltpu.VMEM)
    slab = pltpu.VMEM((6, 36, 8, D), BF)
    out = pl.pallas_call(
        block_kernel,
        in_specs=[pl.BlockSpec(memory_space=pl.ANY)] + [vm] * 7,
        out_specs=vm,
        out_shape=jax.ShapeDtypeStruct((6, 75, 24, D), BF),
        scratch_shapes=[
            pltpu.VMEM((6, 75, 24, D), BF),
            slab, slab, slab, slab,
            slab, pltpu.VMEM((6, 33, 8, D), BF),
            pltpu.VMEM((6, 3, 24, D), BF), pltpu.VMEM((6, 3, 8, D), BF),
            pltpu.VMEM((6 * WIN, D), F32),
            pltpu.VMEM((6 * WIN, 768), BF),
            pltpu.VMEM((2, HEADS * WIN, WIN), F32),
            pltpu.VMEM((2, HEADS * WIN, WIN), BF),
            pltpu.VMEM((6 * WIN, 256), BF),
            pltpu.SemaphoreType.DMA((12,)),
            pltpu.SemaphoreType.DMA((12,)),
            pltpu.SemaphoreType.DMA((2,)),
        ],
        compiler_params=pltpu.CompilerParams(
            collective_id=0, has_side_effects=True, vmem_limit_bytes=34 << 20
        ),
    )(stream, bias, g1.reshape(1, D), wq, wp, g2.reshape(1, D), wup, wdn.T)
    return out[:, :72]


def on_device(
    tokens,
    obs_values,
    obs_dest,
    obs_cell,
    obs_count,
    w_obs,
    ln1_gain,
    w_qkv,
    position_bias,
    w_proj,
    ln2_gain,
    w_up,
    w_down,
):
    levels, lat_rows, lon_cols, features = tokens.shape
    lon_count = lax.axis_size("lon")
    lat_count = lax.axis_size("lat")
    devices = lon_count * lat_count
    row_count = obs_values.shape[0]
    capacity = 2 * row_count // devices
    position = jnp.arange(row_count, dtype=jnp.int32)
    is_live = position < obs_count[0]
    matches = (
        (obs_dest[:, None] == jnp.arange(devices, dtype=jnp.int32)[None, :]) & is_live[:, None]
    ).astype(jnp.int32)
    earlier = jnp.cumsum(matches, axis=0) - matches
    slot_ids = jnp.sum(earlier * matches, axis=1)
    targets = jnp.where(is_live, obs_dest * capacity + slot_ids, devices * capacity)
    buffer = pack(targets, obs_cell, obs_count, obs_values, w_obs)
    received = lax.all_to_all(
        buffer.reshape(devices, capacity, 256), ("lon", "lat"), split_axis=0, concat_axis=0, tiled=True
    )
    stream = scatter(received.reshape(devices * capacity, 256), tokens)
    return block(stream, position_bias, ln1_gain, w_qkv, w_proj, ln2_gain, w_up, w_down)


def solution(mesh):
    in_specs = (
        P(None, "lat", "lon", None),
        P(("lon", "lat"), None),
        P(("lon", "lat")),
        P(("lon", "lat")),
        P(("lon", "lat")),
        P(),
        P(),
        P(),
        P(),
        P(),
        P(),
        P(),
        P(),
    )
    out_specs = P(None, "lat", "lon", None)
    return jax.shard_map(
        on_device, mesh=mesh, in_specs=in_specs, out_specs=out_specs, check_vma=False
    )
```

```python
import math

import jax
import jax.numpy as jnp
import numpy as np
from jax import lax
from jax.experimental import pallas as pl
from jax.experimental.pallas import tpu as pltpu
from jax.sharding import PartitionSpec as P

WZ = 2
WLAT = 6
WLON = 12
F32=jnp.float32; BF=jnp.bfloat16
WIN=144; D=192; HEADS=6; HD=32
NT=(((1,),(1,)),((),()))
LOG2E=math.log2(math.e)

def dot(a,b): return jnp.dot(a,b,preferred_element_type=F32)
def dot_nt(a,b): return lax.dot_general(a,b,NT,preferred_element_type=F32)

def norm(x, gain):
    mean=jnp.mean(x,axis=-1,keepdims=True)
    c=x-mean
    var=jnp.mean(c*c,axis=-1,keepdims=True)
    return (c*lax.rsqrt(var+1e-5)*gain).astype(BF)

def gelu(x):
    h=0.5*x
    return h+h*lax.erf(x*np.float32(math.sqrt(0.5)))

def head_mask(shape, h, width=HD):
    lane=lax.broadcasted_iota(jnp.int32,shape,len(shape)-1)
    return (lane>=h*width)&(lane<(h+1)*width)

GROUPS=((0,4,0),(4,2,128))
MESH=pl.DeviceIdType.MESH

def prep_bias(position_bias):
    b=position_bias*np.float32(LOG2E)
    lvl=np.arange(WIN)//72; row=np.arange(WIN)//12%6
    outs=[]
    for le in range(2):
        for ve in range(2):
            g=2*le*(row>=3)+ve*lvl
            outs.append((g[:,None]!=g[None,:]).astype(np.float32)*np.float32(-1e30))
    return (b[None]+jnp.asarray(np.stack(outs))[:,None]).reshape(4,HEADS*WIN,WIN)


CAP = 32
DEV = 128
BLK = 56
CHUNK = 32
TN = (((0,), (0,)), ((), ()))


def ship_kernel(
    cnt_ref, dest_ref, cell_ref, val_ref, wt_ref, o_ref, y_ref, slot_ref, acc_ref, buf_ref,
    send_sem, recv_sem, local_sem,
):
    n_lat = lax.axis_size("lat")
    n = lax.axis_size("lon") * n_lat
    me = lax.axis_index("lon") * n_lat + lax.axis_index("lat")
    rows = val_ref.shape[0]

    def at(device):
        return (device // n_lat, lax.rem(device, n_lat))

    barrier = pltpu.get_barrier_semaphore()

    def greet(i, _):
        pl.semaphore_signal(
            barrier, inc=1, device_id=at(lax.rem(me + i, n)), device_id_type=MESH
        )
        return 0

    lax.fori_loop(1, n, greet, 0)

    eye = (
        lax.broadcasted_iota(jnp.int32, (8, 64), 0) == lax.broadcasted_iota(jnp.int32, (8, 64), 1)
    ).astype(BF)
    for c in range(0, rows, 512):
        y = dot_nt(val_ref[c : c + 512, :], wt_ref[...])
        cell = cell_ref[0:1, c : c + 512]
        ids = jnp.concatenate(
            [(cell >> 7).astype(F32), (cell & 127).astype(F32), jnp.zeros((6, 512), F32)], axis=0
        ).astype(BF)
        mark = lax.dot_general(ids, eye, TN, preferred_element_type=F32)
        y_ref[c : c + 512, 0:128] = y[:, 0:128].astype(BF)
        y_ref[c : c + 512, 128:256] = jnp.concatenate([y[:, 128:192], mark], axis=1).astype(BF)

    ahead = (
        lax.broadcasted_iota(jnp.int32, (256, 256), 0)
        < lax.broadcasted_iota(jnp.int32, (256, 256), 1)
    ).astype(F32).astype(BF)
    tile = lax.broadcasted_iota(jnp.int32, (DEV, 256), 0)
    carry = jnp.zeros((DEV, 1), F32)
    for c in range(0, rows, 256):
        dest = dest_ref[0:1, c : c + 256]
        live = lax.broadcasted_iota(jnp.int32, (1, 256), 1) + c < cnt_ref[0]
        away = dest - me + jnp.where(dest < me, n, 0)
        away = jnp.where(live, away, -1)
        match = (tile == away).astype(F32)
        before = dot(match.astype(BF), ahead) + carry
        rank = jnp.sum(match * before, axis=0, keepdims=True)
        carry = carry + jnp.sum(match, axis=1, keepdims=True)
        slot_ref[0:1, c : c + 256] = jnp.where(live, away * CAP + rank.astype(jnp.int32), -1)

    def copy_to(i):
        return pltpu.make_async_remote_copy(
            src_ref=buf_ref.at[i], dst_ref=o_ref.at[me],
            send_sem=send_sem.at[i], recv_sem=recv_sem.at[i],
            device_id=at(lax.rem(me + i, n)), device_id_type=MESH,
        )

    def copy_from(i):
        source = lax.rem(me + n - i, n)
        return pltpu.make_async_remote_copy(
            src_ref=buf_ref.at[i], dst_ref=o_ref.at[source],
            send_sem=send_sem.at[i], recv_sem=recv_sem.at[i],
            device_id=at(source), device_id_type=MESH,
        )

    lane = lax.broadcasted_iota(jnp.int32, (16, 128), 1)
    span = CHUNK * CAP
    index = lax.broadcasted_iota(jnp.int32, (span, 256), 0)

    def chunk(c, _):
        for b in range(0, rows, 256):
            hot = (index == slot_ref[0:1, b : b + 256] - c * span).astype(F32).astype(BF)
            part = dot(hot, y_ref[b : b + 256, :])
            if b == 0:
                acc_ref[...] = part
            else:
                acc_ref[...] += part

        def lay(i, _):
            r = pl.multiple_of(i * CAP, CAP)
            block = c * CHUNK + i
            buf_ref[block, 0:32, :] = acc_ref[pl.ds(r, 32), 0:128].astype(BF)
            rest = acc_ref[pl.ds(r, 32), 128:256]
            buf_ref[block, 32:48, :] = jnp.where(
                lane < 64, rest[0:16], pltpu.roll(rest[16:32], 64, 1)
            ).astype(BF)
            marks = jnp.zeros((8, 128), F32)
            for g in range(4):
                marks = jnp.where(
                    lane[:8] // 2 == g, pltpu.roll(rest[8 * g : 8 * g + 8], 64 + 2 * g, 1), marks
                )
            buf_ref[block, 48:56, :] = marks.astype(BF)
            return 0

        lax.fori_loop(0, CHUNK, lay, 0, unroll=4)

        @pl.when(c == 0)
        def _():
            pl.semaphore_wait(barrier, n - 1)

        def send(i, _):
            copy_to(c * CHUNK + i).start()
            return 0

        lax.fori_loop(jnp.where(c == 0, 1, 0), CHUNK, send, 0)
        return 0

    lax.fori_loop(0, DEV // CHUNK, chunk, 0)
    local = pltpu.make_async_copy(buf_ref.at[0], o_ref.at[me], local_sem)
    local.start()

    def land(i, _):
        copy_from(i).wait_recv()
        return 0

    lax.fori_loop(1, n, land, 0)

    def sent(i, _):
        copy_to(i).wait_send()
        return 0

    lax.fori_loop(1, n, sent, 0)
    local.wait()


def ship(obs_dest, obs_cell, obs_count, values, w_obs):
    rows = values.shape[0]
    sm = pl.BlockSpec(memory_space=pltpu.SMEM)
    vm = pl.BlockSpec(memory_space=pltpu.VMEM)
    return pl.pallas_call(
        ship_kernel,
        in_specs=[sm, vm, vm, vm, vm],
        out_specs=vm,
        out_shape=jax.ShapeDtypeStruct((DEV, BLK, 128), BF),
        scratch_shapes=[
            pltpu.VMEM((rows, 256), BF),
            pltpu.VMEM((1, rows), jnp.int32),
            pltpu.VMEM((CHUNK * CAP, 256), F32),
            pltpu.VMEM((DEV, BLK, 128), BF),
            pltpu.SemaphoreType.DMA((DEV,)),
            pltpu.SemaphoreType.DMA((DEV,)),
            pltpu.SemaphoreType.DMA,
        ],
        compiler_params=pltpu.CompilerParams(
            collective_id=1, has_side_effects=True, vmem_limit_bytes=20 << 20
        ),
    )(obs_count, obs_dest.reshape(1, rows), obs_cell.reshape(1, rows), values, w_obs.T)


def scatter_kernel(recv_ref, tok_ref, out_ref, rows, ids_v, ids_s, sem, *accs):
    cells = tok_ref.shape[0]
    group = lax.broadcasted_iota(jnp.int32, (8, 128), 0)
    lane = lax.broadcasted_iota(jnp.int32, (8, 128), 1)
    sel = jnp.where(lane == 2 * group, 128.0, jnp.where(lane == 2 * group + 1, 1.0, 0.0)).astype(BF)
    for b in range(8):
        marks = recv_ref[16 * b : 16 * b + 16, 48:56, :].astype(F32).reshape(128, 128).astype(BF)
        ids_v[:, 128 * b : 128 * b + 128] = (dot_nt(sel, marks) + 0.5).astype(jnp.int32)
    cp = pltpu.make_async_copy(ids_v, ids_s, sem)
    cp.start()

    def prep(d, _):
        r = pl.multiple_of(d * 64, 64)
        rows[pl.ds(r, 32, stride=2), :] = recv_ref[d, 0:32, :].astype(F32)
        rest = recv_ref[d, 32:48, :].astype(F32)
        rows[pl.ds(r + 1, 16, stride=2), :] = rest
        rows[pl.ds(r + 33, 16, stride=2), :] = pltpu.roll(rest, 64, 1)
        return 0

    lax.fori_loop(0, DEV, prep, 0, unroll=4)

    def init(g, _):
        r = pl.multiple_of(g * 144, 144)
        t = tok_ref[pl.ds(r, 144), :].astype(F32)
        accs[0][pl.ds(2 * r, 144, stride=2), :] = t[:, 0:128]
        accs[0][pl.ds(2 * r + 1, 144, stride=2), 0:64] = t[:, 128:192]
        for a in accs[1:]:
            a[pl.ds(2 * r, 288), :] = jnp.zeros((288, 128), F32)
        return 0

    lax.fori_loop(0, cells // 144, init, 0)
    cp.wait()
    half = DEV // len(accs)

    def body(d, _):
        for j in range(CAP):
            for a, acc in enumerate(accs):
                src = d + a * half
                c = ids_s[j // 8, src * 8 + j % 8]
                acc[pl.ds(2 * c, 2), :] = (
                    acc[pl.ds(2 * c, 2), :] + rows[pl.ds(2 * (src * CAP + j), 2), :]
                )
        return 0

    lax.fori_loop(0, half, body, 0)

    def fin(g, _):
        r = pl.multiple_of(g * 144, 144)
        t = accs[0][pl.ds(2 * r, 144, stride=2), :]
        for a in accs[1:]:
            t = t + a[pl.ds(2 * r, 144, stride=2), :]
        out_ref[pl.ds(r, 144), 0:128] = t.astype(BF)
        t = accs[0][pl.ds(2 * r + 1, 144, stride=2), :]
        for a in accs[1:]:
            t = t + a[pl.ds(2 * r + 1, 144, stride=2), :]
        out_ref[pl.ds(r, 144), 128:192] = t[:, 0:64].astype(BF)
        return 0

    lax.fori_loop(0, cells // 144, fin, 0)


def scatter(recv, tokens):
    cells = 6 * 72 * 24
    vm = pl.BlockSpec(memory_space=pltpu.VMEM)
    out = pl.pallas_call(
        scatter_kernel,
        in_specs=[vm, vm],
        out_specs=vm,
        out_shape=jax.ShapeDtypeStruct((cells, D), BF),
        scratch_shapes=[
            pltpu.VMEM((2 * DEV * CAP, 128), F32),
            pltpu.VMEM((8, 1024), jnp.int32),
            pltpu.SMEM((8, 1024), jnp.int32),
            pltpu.SemaphoreType.DMA,
            pltpu.VMEM((2 * cells, 128), F32),
            pltpu.VMEM((2 * cells, 128), F32),
        ],
        compiler_params=pltpu.CompilerParams(vmem_limit_bytes=30 << 20),
    )(recv, tokens.reshape(cells, D))
    return out.reshape(tokens.shape)


def attend(xs, qkv_ref, s_ref, p_ref, ctx_ref, bias_ref, variants, g1_ref, wqkv_ref, wp_ref, g2_ref, wup_ref, wdnt_ref):
    zero = jnp.zeros((), BF)
    count = len(variants)
    n1 = norm(xs[...], g1_ref[...])
    qkv_ref[:, 0:256] = (
        dot(n1, wqkv_ref[:, 0:256]) * np.float32(LOG2E / math.sqrt(HD))
    ).astype(BF)
    qkv_ref[:, 256:512] = dot(n1, wqkv_ref[:, 256:512]).astype(BF)
    qkv_ref[:, 512:768] = dot(n1, wqkv_ref[:, 512:768]).astype(BF)

    def scores(w):
        sl = slice(w * WIN, (w + 1) * WIN)
        for h0, nh, l0 in GROUPS:
            qg = qkv_ref[sl, l0 : l0 + 128]
            kg = qkv_ref[sl, 256 + l0 : 384 + l0]
            qs = jnp.concatenate(
                [jnp.where(head_mask((WIN, 128), h), qg, zero) for h in range(nh)], axis=0
            )
            s_ref[w % 2, h0 * WIN : (h0 + nh) * WIN, :] = dot_nt(qs, kg)

    def softmax(w):
        sl = slice(w * WIN, (w + 1) * WIN)
        sums = []
        for h in range(HEADS):
            rows = slice(h * WIN, (h + 1) * WIN)
            s = s_ref[w % 2, rows, :] + bias_ref[variants[w], rows, :]
            p = jnp.exp2(s - jnp.max(s, axis=-1, keepdims=True))
            sums.append(jnp.sum(p, axis=-1, keepdims=True))
            p_ref[w % 2, rows, :] = p.astype(BF)
        for h0, nh, l0 in GROUPS:
            o = dot(p_ref[w % 2, h0 * WIN : (h0 + nh) * WIN, :], qkv_ref[sl, 512 + l0 : 640 + l0])
            c = o[:WIN]
            total = sums[h0] * jnp.ones((1, 128), F32)
            for h in range(1, nh):
                mask = head_mask((WIN, 128), h)
                c = jnp.where(mask, o[h * WIN : (h + 1) * WIN], c)
                total = jnp.where(mask, sums[h0 + h], total)
            ctx_ref[sl, l0 : l0 + 128] = (c * (1.0 / total)).astype(BF)

    scores(0)
    for w in range(count):
        if w + 1 < count:
            scores(w + 1)
        softmax(w)
    att = (xs[...] + dot(ctx_ref[:, :D], wp_ref[...])).astype(BF).astype(F32)
    n2 = norm(att, g2_ref[...])
    acc = att
    for j in range(3):
        hid = gelu(dot(n2, wup_ref[:, j * 256 : (j + 1) * 256])).astype(BF)
        acc = acc + dot_nt(hid, wdnt_ref[:, j * 256 : (j + 1) * 256])
    xs[...] = acc


def block_kernel(
    x_hbm, bias_ref, g1_ref, wqkv_ref, wp_ref, g2_ref, wup_ref, wdnt_ref, o_ref,
    xe, from_right, from_left, to_right, to_left, back_left, back_right, back_lat, back_diag,
    xs, qkv_ref, s_ref, p_ref, ctx_ref, send_sem, recv_sem, local_sem,
):
    lon = lax.axis_index("lon")
    lat = lax.axis_index("lat")
    n_lon = lax.axis_size("lon")
    n_lat = lax.axis_size("lat")
    east = lax.rem(lon + 1, n_lon)
    west = lax.rem(lon + n_lon - 1, n_lon)
    north = lax.rem(lat + 1, n_lat)
    south = lax.rem(lat + n_lat - 1, n_lat)

    locals_ = [
        pltpu.make_async_copy(
            x_hbm.at[:, r0:r1], xe.at[:, r0:r1], local_sem.at[n]
        )
        for n, (r0, r1) in enumerate(((0, 39), (39, 72)))
    ]
    for copy in locals_:
        copy.start()

    barrier = pltpu.get_barrier_semaphore()
    partners = ((east, lat), (west, lat), (lon, north), (lon, south), (east, south), (west, north))
    for partner in partners:
        pl.semaphore_signal(barrier, inc=1, device_id=partner, device_id_type=MESH)
    pl.semaphore_wait(barrier, len(partners))

    def remote(n, src, dst, target):
        return pltpu.make_async_remote_copy(
            src_ref=src, dst_ref=dst, send_sem=send_sem.at[n], recv_sem=recv_sem.at[n],
            device_id=target, device_id_type=MESH,
        )

    halo = [
        remote(0, x_hbm.at[:, 3:39, 0:8], from_right, (west, lat)),
        remote(1, x_hbm.at[:, 39:72, 16:24], from_left.at[:, 0:33], (east, lat)),
        remote(2, x_hbm.at[:, 0:3], xe.at[:, 72:75], (lon, south)),
        remote(3, x_hbm.at[:, 0:3, 16:24], from_left.at[:, 33:36], (east, south)),
    ]
    home_east = [
        remote(4 + j, to_right.at[:, 12 * j : 12 * j + 12], back_left.at[:, 12 * j : 12 * j + 12], (east, lat))
        for j in range(3)
    ]
    home_west = [
        remote(7 + j, to_left.at[:, 12 * j : end], back_right.at[:, 12 * j : end], (west, lat))
        for j, end in enumerate((12, 24, 33))
    ]
    home_diag = remote(10, to_left.at[:, 33:36], back_diag, (west, north))
    home_lat = remote(11, o_ref.at[:, 72:75], back_lat, (lon, north))
    for copy in halo:
        copy.start()
    locals_[0].wait()

    def step(s, _):
        phase = s // 3
        turn = lax.rem(s, 3)
        j = jnp.where(phase < 2, turn, 5 - turn)
        inner = (phase == 0) | (phase == 3)

        @pl.when(s == 3)
        def _():
            halo[0].wait_recv()

        @pl.when(s == 6)
        def _():
            locals_[1].wait()
            for copy in halo[1:]:
                copy.wait_recv()

        def places():
            for w in range(6):
                for i in range(2):
                    for r in range(6):
                        level = (w // 2 * 2 + 1 + i) % 6
                        yield level, 3 + 6 * (2 * j + w % 2) + r, w * WIN + (i * 6 + r) * 12

        @pl.when(inner)
        def _():
            for level, row, at in places():
                xs[at : at + 12, :] = xe[level, row].astype(F32)[6:18]

        @pl.when(phase == 1)
        def _():
            for level, row, at in places():
                xs[at : at + 6, :] = xe[level, row, 16:24].astype(F32)[2:8]
                xs[at + 6 : at + 12, :] = from_right[level, row - 3].astype(F32)[0:6]

        @pl.when(phase == 2)
        def _():
            for level, row, at in places():
                xs[at : at + 6, :] = from_left[level, row - 39].astype(F32)[2:8]
                xs[at + 6 : at + 12, :] = xe[level, row, 0:8].astype(F32)[0:6]

        lat_edge = ((j == 5) & (lat == n_lat - 1)).astype(jnp.int32)
        variants = [w // 4 + (2 * lat_edge if w % 2 else 0) for w in range(6)]
        attend(
            xs, qkv_ref, s_ref, p_ref, ctx_ref, bias_ref, variants,
            g1_ref, wqkv_ref, wp_ref, g2_ref, wup_ref, wdnt_ref,
        )

        @pl.when(inner)
        def _():
            for level, row, at in places():
                o_ref[level, row, 6:18, :] = xs[at : at + 12, :].astype(BF)

        @pl.when(phase == 1)
        def _():
            for level, row, at in places():
                o_ref[level, row, 18:24, :] = xs[at : at + 6, :].astype(BF)
                to_right[level, row - 3, 0:6, :] = xs[at + 6 : at + 12, :].astype(BF)

        @pl.when(phase == 2)
        def _():
            for level, row, at in places():
                to_left[level, row - 39, 2:8, :] = xs[at : at + 6, :].astype(BF)
                o_ref[level, row, 0:6, :] = xs[at + 6 : at + 12, :].astype(BF)

        for n in range(3):
            @pl.when(s == 3 + n)
            def _(n=n):
                home_east[n].start()

            @pl.when(s == 6 + n)
            def _(n=n):
                home_west[2 - n].start()
                if n == 0:
                    home_diag.start()

        @pl.when(s == 9)
        def _():
            home_lat.start()

        return 0

    lax.fori_loop(0, 12, step, 0)
    for copy in home_east:
        copy.wait_recv()
    home_lat.wait_recv()
    home_diag.wait_recv()
    for copy in home_west:
        copy.wait_recv()

    def merge(level, _):
        for r in range(36):
            o_ref[level, 3 + r, 0:6, :] = back_left[level, r, 0:6, :]
        for r in range(33):
            o_ref[level, 39 + r, 18:24, :] = back_right[level, r, 2:8, :]
        for r in range(3):
            o_ref[level, r, 0:18, :] = back_lat[level, r, 0:18, :]
            o_ref[level, r, 18:24, :] = back_diag[level, r, 2:8, :]
        return 0

    lax.fori_loop(0, 6, merge, 0)
    for copy in (*halo, *home_east, *home_west, home_diag, home_lat):
        copy.wait_send()


def block(stream, position_bias, g1, wqkv, wp, g2, wup, wdn):
    bias = prep_bias(position_bias)
    wq = jnp.pad(wqkv.reshape(D, 3, D), ((0, 0), (0, 0), (0, 64))).reshape(D, 768)
    vm = pl.BlockSpec(memory_space=pltpu.VMEM)
    slab = pltpu.VMEM((6, 36, 8, D), BF)
    out = pl.pallas_call(
        block_kernel,
        in_specs=[pl.BlockSpec(memory_space=pl.ANY)] + [vm] * 7,
        out_specs=vm,
        out_shape=jax.ShapeDtypeStruct((6, 75, 24, D), BF),
        scratch_shapes=[
            pltpu.VMEM((6, 75, 24, D), BF),
            slab, slab, slab, slab,
            slab, pltpu.VMEM((6, 33, 8, D), BF),
            pltpu.VMEM((6, 3, 24, D), BF), pltpu.VMEM((6, 3, 8, D), BF),
            pltpu.VMEM((6 * WIN, D), F32),
            pltpu.VMEM((6 * WIN, 768), BF),
            pltpu.VMEM((2, HEADS * WIN, WIN), F32),
            pltpu.VMEM((2, HEADS * WIN, WIN), BF),
            pltpu.VMEM((6 * WIN, 256), BF),
            pltpu.SemaphoreType.DMA((12,)),
            pltpu.SemaphoreType.DMA((12,)),
            pltpu.SemaphoreType.DMA((2,)),
        ],
        compiler_params=pltpu.CompilerParams(
            collective_id=0, has_side_effects=True, vmem_limit_bytes=34 << 20
        ),
    )(stream, bias, g1.reshape(1, D), wq, wp, g2.reshape(1, D), wup, wdn.T)
    return out[:, :72]


def on_device(
    tokens,
    obs_values,
    obs_dest,
    obs_cell,
    obs_count,
    w_obs,
    ln1_gain,
    w_qkv,
    position_bias,
    w_proj,
    ln2_gain,
    w_up,
    w_down,
):
    received = ship(obs_dest, obs_cell, obs_count, obs_values, w_obs)
    stream = scatter(received, tokens)
    return block(stream, position_bias, ln1_gain, w_qkv, w_proj, ln2_gain, w_up, w_down)


def solution(mesh):
    in_specs = (
        P(None, "lat", "lon", None),
        P(("lon", "lat"), None),
        P(("lon", "lat")),
        P(("lon", "lat")),
        P(("lon", "lat")),
        P(),
        P(),
        P(),
        P(),
        P(),
        P(),
        P(),
        P(),
    )
    out_specs = P(None, "lat", "lon", None)
    return jax.shard_map(
        on_device, mesh=mesh, in_specs=in_specs, out_specs=out_specs, check_vma=False
    )
```

```python
import math

import jax
import jax.numpy as jnp
import numpy as np
from jax import lax
from jax.experimental import pallas as pl
from jax.experimental.pallas import tpu as pltpu
from jax.sharding import PartitionSpec as P

WZ = 2
WLAT = 6
WLON = 12
F32=jnp.float32; BF=jnp.bfloat16
WIN=144; D=192; HEADS=6; HD=32
NT=(((1,),(1,)),((),()))
LOG2E=math.log2(math.e)

def dot(a,b): return jnp.dot(a,b,preferred_element_type=F32)
def dot_nt(a,b): return lax.dot_general(a,b,NT,preferred_element_type=F32)

def norm(x, gain):
    mean=jnp.mean(x,axis=-1,keepdims=True)
    c=x-mean
    var=jnp.mean(c*c,axis=-1,keepdims=True)
    return (c*lax.rsqrt(var+1e-5)*gain).astype(BF)

def gelu(x):
    h=0.5*x
    return h+h*lax.erf(x*np.float32(math.sqrt(0.5)))

def head_mask(shape, h, width=HD):
    lane=lax.broadcasted_iota(jnp.int32,shape,len(shape)-1)
    return (lane>=h*width)&(lane<(h+1)*width)

GROUPS=((0,4,0),(4,2,128))
MESH=pl.DeviceIdType.MESH

def mask_rows(axis):
    at = lax.broadcasted_iota(jnp.int32, (WIN, WIN), axis)
    upper = at >= 72
    return upper, ((at >= 36) & (at < 72)) | (at >= 108)


def fill_bias(raw_ref, bias_ref):
    level_q, lat_q = mask_rows(0)
    level_k, lat_k = mask_rows(1)
    zero = jnp.zeros((WIN, WIN), F32)
    level_cut = jnp.where(level_q != level_k, -1e30, zero)
    lat_cut = jnp.where(lat_q != lat_k, -1e30, zero)
    both_cut = jnp.where((level_q != level_k) | (lat_q != lat_k), -1e30, zero)

    def head(h, _):
        rows = pl.ds(pl.multiple_of(h * WIN, WIN), WIN)
        b = raw_ref[rows, :] * np.float32(LOG2E)
        for v, cut in enumerate((zero, level_cut, lat_cut, both_cut)):
            bias_ref[v, rows, :] = b + cut
        return 0

    lax.fori_loop(0, HEADS, head, 0)


CAP = 32
DEV = 128
BLK = 56
CHUNK = 32
TN = (((0,), (0,)), ((), ()))


def ship_kernel(
    cnt_ref, dest_ref, cell_ref, val_ref, wt_ref, o_ref, y_ref, slot_ref, acc_ref, buf_ref,
    send_sem, recv_sem, local_sem,
):
    n_lat = lax.axis_size("lat")
    n = lax.axis_size("lon") * n_lat
    me = lax.axis_index("lon") * n_lat + lax.axis_index("lat")
    rows = val_ref.shape[0]

    def at(device):
        return (device // n_lat, lax.rem(device, n_lat))

    barrier = pltpu.get_barrier_semaphore()

    def greet(i, _):
        pl.semaphore_signal(
            barrier, inc=1, device_id=at(lax.rem(me + i, n)), device_id_type=MESH
        )
        return 0

    lax.fori_loop(1, n, greet, 0)

    eye = (
        lax.broadcasted_iota(jnp.int32, (8, 64), 0) == lax.broadcasted_iota(jnp.int32, (8, 64), 1)
    ).astype(BF)
    for c in range(0, rows, 512):
        y = dot_nt(val_ref[c : c + 512, :], wt_ref[...])
        cell = cell_ref[0:1, c : c + 512]
        ids = jnp.concatenate(
            [(cell >> 7).astype(F32), (cell & 127).astype(F32), jnp.zeros((6, 512), F32)], axis=0
        ).astype(BF)
        mark = lax.dot_general(ids, eye, TN, preferred_element_type=F32)
        y_ref[c : c + 512, 0:128] = y[:, 0:128].astype(BF)
        y_ref[c : c + 512, 128:256] = jnp.concatenate([y[:, 128:192], mark], axis=1).astype(BF)

    ahead = (
        lax.broadcasted_iota(jnp.int32, (256, 256), 0)
        < lax.broadcasted_iota(jnp.int32, (256, 256), 1)
    ).astype(F32).astype(BF)
    tile = lax.broadcasted_iota(jnp.int32, (DEV, 256), 0)
    carry = jnp.zeros((DEV, 1), F32)
    for c in range(0, rows, 256):
        dest = dest_ref[0:1, c : c + 256]
        live = lax.broadcasted_iota(jnp.int32, (1, 256), 1) + c < cnt_ref[0]
        away = dest - me + jnp.where(dest < me, n, 0)
        away = jnp.where(live, away, -1)
        match = (tile == away).astype(F32)
        before = dot(match.astype(BF), ahead) + carry
        rank = jnp.sum(match * before, axis=0, keepdims=True)
        carry = carry + jnp.sum(match, axis=1, keepdims=True)
        slot_ref[0:1, c : c + 256] = jnp.where(live, away * CAP + rank.astype(jnp.int32), -1)

    def copy_to(i):
        return pltpu.make_async_remote_copy(
            src_ref=buf_ref.at[i], dst_ref=o_ref.at[me],
            send_sem=send_sem.at[i], recv_sem=recv_sem.at[i],
            device_id=at(lax.rem(me + i, n)), device_id_type=MESH,
        )

    def copy_from(i):
        source = lax.rem(me + n - i, n)
        return pltpu.make_async_remote_copy(
            src_ref=buf_ref.at[i], dst_ref=o_ref.at[source],
            send_sem=send_sem.at[i], recv_sem=recv_sem.at[i],
            device_id=at(source), device_id_type=MESH,
        )

    lane = lax.broadcasted_iota(jnp.int32, (16, 128), 1)
    span = CHUNK * CAP
    index = lax.broadcasted_iota(jnp.int32, (span, 256), 0)

    def chunk(c, _):
        for b in range(0, rows, 256):
            hot = (index == slot_ref[0:1, b : b + 256] - c * span).astype(F32).astype(BF)
            part = dot(hot, y_ref[b : b + 256, :])
            if b == 0:
                acc_ref[...] = part
            else:
                acc_ref[...] += part

        def lay(i, _):
            r = pl.multiple_of(i * CAP, CAP)
            block = c * CHUNK + i
            buf_ref[block, 0:32, :] = acc_ref[pl.ds(r, 32), 0:128].astype(BF)
            rest = acc_ref[pl.ds(r, 32), 128:256]
            buf_ref[block, 32:48, :] = jnp.where(
                lane < 64, rest[0:16], pltpu.roll(rest[16:32], 64, 1)
            ).astype(BF)
            marks = jnp.zeros((8, 128), F32)
            for g in range(4):
                marks = jnp.where(
                    lane[:8] // 2 == g, pltpu.roll(rest[8 * g : 8 * g + 8], 64 + 2 * g, 1), marks
                )
            buf_ref[block, 48:56, :] = marks.astype(BF)
            return 0

        lax.fori_loop(0, CHUNK, lay, 0, unroll=4)

        @pl.when(c == 0)
        def _():
            pl.semaphore_wait(barrier, n - 1)

        def send(i, _):
            copy_to(c * CHUNK + i).start()
            return 0

        lax.fori_loop(jnp.where(c == 0, 1, 0), CHUNK, send, 0)
        return 0

    lax.fori_loop(0, DEV // CHUNK, chunk, 0)
    local = pltpu.make_async_copy(buf_ref.at[0], o_ref.at[me], local_sem)
    local.start()

    def land(i, _):
        copy_from(i).wait_recv()
        return 0

    lax.fori_loop(1, n, land, 0)

    def sent(i, _):
        copy_to(i).wait_send()
        return 0

    lax.fori_loop(1, n, sent, 0)
    local.wait()


def ship(obs_dest, obs_cell, obs_count, values, w_obs):
    rows = values.shape[0]
    sm = pl.BlockSpec(memory_space=pltpu.SMEM)
    vm = pl.BlockSpec(memory_space=pltpu.VMEM)
    return pl.pallas_call(
        ship_kernel,
        in_specs=[sm, vm, vm, vm, vm],
        out_specs=vm,
        out_shape=jax.ShapeDtypeStruct((DEV, BLK, 128), BF),
        scratch_shapes=[
            pltpu.VMEM((rows, 256), BF),
            pltpu.VMEM((1, rows), jnp.int32),
            pltpu.VMEM((CHUNK * CAP, 256), F32),
            pltpu.VMEM((DEV, BLK, 128), BF),
            pltpu.SemaphoreType.DMA((DEV,)),
            pltpu.SemaphoreType.DMA((DEV,)),
            pltpu.SemaphoreType.DMA,
        ],
        compiler_params=pltpu.CompilerParams(
            collective_id=1, has_side_effects=True, vmem_limit_bytes=20 << 20
        ),
    )(obs_count, obs_dest.reshape(1, rows), obs_cell.reshape(1, rows), values, w_obs.T)


def scatter_kernel(recv_ref, tok_ref, out_ref, rows, ids_v, ids_s, sem, *accs):
    cells = tok_ref.shape[0]
    group = lax.broadcasted_iota(jnp.int32, (8, 128), 0)
    lane = lax.broadcasted_iota(jnp.int32, (8, 128), 1)
    sel = jnp.where(lane == 2 * group, 128.0, jnp.where(lane == 2 * group + 1, 1.0, 0.0)).astype(BF)
    for b in range(8):
        marks = recv_ref[16 * b : 16 * b + 16, 48:56, :].astype(F32).reshape(128, 128).astype(BF)
        ids_v[:, 128 * b : 128 * b + 128] = 2 * (dot_nt(sel, marks) + 0.5).astype(jnp.int32)
    cp = pltpu.make_async_copy(ids_v, ids_s, sem)
    cp.start()

    def prep(d, _):
        r = pl.multiple_of(d * 64, 64)
        rows[pl.ds(r, 32, stride=2), :] = recv_ref[d, 0:32, :].astype(F32)
        rest = recv_ref[d, 32:48, :].astype(F32)
        rows[pl.ds(r + 1, 16, stride=2), :] = rest
        rows[pl.ds(r + 33, 16, stride=2), :] = pltpu.roll(rest, 64, 1)
        return 0

    lax.fori_loop(0, DEV, prep, 0, unroll=4)

    def init(g, _):
        r = pl.multiple_of(g * 144, 144)
        t = tok_ref[pl.ds(r, 144), :].astype(F32)
        accs[0][pl.ds(2 * r, 144, stride=2), :] = t[:, 0:128]
        accs[0][pl.ds(2 * r + 1, 144, stride=2), 0:64] = t[:, 128:192]
        for a in accs[1:]:
            a[pl.ds(2 * r, 288), :] = jnp.zeros((288, 128), F32)
        return 0

    lax.fori_loop(0, cells // 144, init, 0)
    cp.wait()
    half = DEV // len(accs)

    def body(d, _):
        for j in range(0, CAP, 2):
            for a, acc in enumerate(accs):
                src = d + a * half
                first = ids_s[j // 8, src * 8 + j % 8]
                second = ids_s[(j + 1) // 8, src * 8 + (j + 1) % 8]
                row = 2 * (src * CAP + j)
                old = acc[pl.ds(second, 2), :]
                new = acc[pl.ds(first, 2), :] + rows[pl.ds(row, 2), :]
                old = jnp.where(first == second, new, old)
                acc[pl.ds(first, 2), :] = new
                acc[pl.ds(second, 2), :] = old + rows[pl.ds(row + 2, 2), :]
        return 0

    lax.fori_loop(0, half, body, 0)

    def fin(g, _):
        r = pl.multiple_of(g * 144, 144)
        t = accs[0][pl.ds(2 * r, 144, stride=2), :]
        for a in accs[1:]:
            t = t + a[pl.ds(2 * r, 144, stride=2), :]
        out_ref[pl.ds(r, 144), 0:128] = t.astype(BF)
        t = accs[0][pl.ds(2 * r + 1, 144, stride=2), :]
        for a in accs[1:]:
            t = t + a[pl.ds(2 * r + 1, 144, stride=2), :]
        out_ref[pl.ds(r, 144), 128:192] = t[:, 0:64].astype(BF)
        return 0

    lax.fori_loop(0, cells // 144, fin, 0)


def scatter(recv, tokens):
    cells = 6 * 72 * 24
    vm = pl.BlockSpec(memory_space=pltpu.VMEM)
    out = pl.pallas_call(
        scatter_kernel,
        in_specs=[vm, vm],
        out_specs=vm,
        out_shape=jax.ShapeDtypeStruct((cells, D), BF),
        scratch_shapes=[
            pltpu.VMEM((2 * DEV * CAP, 128), F32),
            pltpu.VMEM((8, 1024), jnp.int32),
            pltpu.SMEM((8, 1024), jnp.int32),
            pltpu.SemaphoreType.DMA,
            pltpu.VMEM((2 * cells, 128), F32),
            pltpu.VMEM((2 * cells, 128), F32),
        ],
        compiler_params=pltpu.CompilerParams(vmem_limit_bytes=30 << 20),
    )(recv, tokens.reshape(cells, D))
    return out.reshape(tokens.shape)


def attend(xs, qkv_ref, s_ref, p_ref, ctx_ref, bias_ref, variants, g1_ref, wqkv_ref, wk_ref, wp_ref, g2_ref, wup_ref, wdnt_ref):
    zero = jnp.zeros((), BF)
    count = len(variants)
    n1 = norm(xs[...], g1_ref[...])
    qkv_ref[:, 0:256] = (
        dot(n1, wqkv_ref[:, 0:256]) * np.float32(LOG2E / math.sqrt(HD))
    ).astype(BF)
    qkv_ref[:, 256:512] = dot(n1, wk_ref[...]).astype(BF)
    qkv_ref[:, 512:704] = dot(n1, wqkv_ref[:, 384:576]).astype(BF)

    def scores(w):
        sl = slice(w * WIN, (w + 1) * WIN)
        for h0, nh, l0 in GROUPS:
            qg = qkv_ref[sl, l0 : l0 + 128]
            kg = qkv_ref[sl, 256 + l0 : 384 + l0]
            qs = jnp.concatenate(
                [jnp.where(head_mask((WIN, 128), h), qg, zero) for h in range(nh)], axis=0
            )
            s_ref[w % 2, h0 * WIN : (h0 + nh) * WIN, :] = dot_nt(qs, kg)

    def softmax(w):
        sl = slice(w * WIN, (w + 1) * WIN)
        sums = []
        for h in range(HEADS):
            rows = slice(h * WIN, (h + 1) * WIN)
            s = s_ref[w % 2, rows, :] + bias_ref[variants[w], rows, :]
            p = jnp.exp2(s - jnp.max(s, axis=-1, keepdims=True))
            sums.append(jnp.sum(p, axis=-1, keepdims=True))
            p_ref[w % 2, rows, :] = p.astype(BF)
        for h0, nh, l0 in GROUPS:
            o = dot(p_ref[w % 2, h0 * WIN : (h0 + nh) * WIN, :], qkv_ref[sl, 512 + l0 : 640 + l0])
            c = o[:WIN]
            total = sums[h0] * jnp.ones((1, 128), F32)
            for h in range(1, nh):
                mask = head_mask((WIN, 128), h)
                c = jnp.where(mask, o[h * WIN : (h + 1) * WIN], c)
                total = jnp.where(mask, sums[h0 + h], total)
            ctx_ref[sl, l0 : l0 + 128] = (c * (1.0 / total)).astype(BF)

    scores(0)
    for w in range(count):
        if w + 1 < count:
            scores(w + 1)
        softmax(w)
    att = (xs[...] + dot(ctx_ref[:, :D], wp_ref[...])).astype(BF).astype(F32)
    n2 = norm(att, g2_ref[...])
    acc = att
    for j in range(3):
        hid = gelu(dot(n2, wup_ref[:, j * 256 : (j + 1) * 256])).astype(BF)
        acc = acc + dot_nt(hid, wdnt_ref[:, j * 256 : (j + 1) * 256])
    xs[...] = acc


def block_kernel(
    x_ref, raw_ref, g1_ref, wqkv_ref, wp_ref, g2_ref, wup_ref, wdnt_ref, o_ref,
    near, from_right, from_left, to_right, to_left, back_left, back_right, back_lat, back_diag,
    xs, qkv_ref, s_ref, p_ref, ctx_ref, bias_ref, wk_ref, send_sem, recv_sem,
):
    lon = lax.axis_index("lon")
    lat = lax.axis_index("lat")
    n_lon = lax.axis_size("lon")
    n_lat = lax.axis_size("lat")
    east = lax.rem(lon + 1, n_lon)
    west = lax.rem(lon + n_lon - 1, n_lon)
    north = lax.rem(lat + 1, n_lat)
    south = lax.rem(lat + n_lat - 1, n_lat)

    barrier = pltpu.get_barrier_semaphore()
    partners = ((east, lat), (west, lat), (lon, north), (lon, south), (east, south), (west, north))
    for partner in partners:
        pl.semaphore_signal(barrier, inc=1, device_id=partner, device_id_type=MESH)
    fill_bias(raw_ref, bias_ref)
    wk_ref[...] = pltpu.roll(wqkv_ref[:, 128:384].astype(F32), 192, 1).astype(BF)
    qkv_ref[:, 704:768] = jnp.zeros((6 * WIN, 64), BF)
    pl.semaphore_wait(barrier, len(partners))

    def remote(n, src, dst, target):
        return pltpu.make_async_remote_copy(
            src_ref=src, dst_ref=dst, send_sem=send_sem.at[n], recv_sem=recv_sem.at[n],
            device_id=target, device_id_type=MESH,
        )

    halo = [
        remote(0, x_ref.at[:, 3:39, 0:8], from_right, (west, lat)),
        remote(1, x_ref.at[:, 39:72, 16:24], from_left.at[:, 0:33], (east, lat)),
        remote(2, x_ref.at[:, 0:3], near, (lon, south)),
        remote(3, x_ref.at[:, 0:3, 16:24], from_left.at[:, 33:36], (east, south)),
    ]
    home_east = [
        remote(4 + j, to_right.at[:, 12 * j : 12 * j + 12], back_left.at[:, 12 * j : 12 * j + 12], (east, lat))
        for j in range(3)
    ]
    home_west = [
        remote(7 + j, to_left.at[:, 12 * j : end], back_right.at[:, 12 * j : end], (west, lat))
        for j, end in enumerate((12, 24, 33))
    ]
    home_diag = remote(10, to_left.at[:, 33:36], back_diag, (west, north))
    home_lat = remote(11, o_ref.at[:, 72:75], back_lat, (lon, north))
    for copy in halo:
        copy.start()

    def step(s, _):
        phase = s // 3
        turn = lax.rem(s, 3)
        j = jnp.where(phase < 2, turn, 5 - turn)
        inner = (phase == 0) | (phase == 3)

        @pl.when(s == 3)
        def _():
            halo[0].wait_recv()

        @pl.when(s == 6)
        def _():
            for copy in halo[1:]:
                copy.wait_recv()

        def places(last=None):
            for w in range(6):
                for i in range(2):
                    for r in range(6):
                        if last is not None and last != (w % 2 == 1 and r >= 3):
                            continue
                        level = (w // 2 * 2 + 1 + i) % 6
                        row = 3 + 6 * (2 * j + w % 2) + r
                        yield level, row, w * WIN + (i * 6 + r) * 12, r - 3

        def load_inner(level, row, at, source):
            xs[at : at + 12, :] = source[level, row].astype(F32)[6:18]

        def load_left(level, row, at, source):
            xs[at + 6 : at + 12, :] = source[level, row, 0:8].astype(F32)[0:6]

        for wanted, load in ((inner, load_inner), (phase == 2, load_left)):
            @pl.when(wanted)
            def _(load=load):
                for level, row, at, _ in places(False):
                    load(level, row, at, x_ref)

            @pl.when(wanted & (j < 5))
            def _(load=load):
                for level, row, at, _ in places(True):
                    load(level, row, at, x_ref)

            @pl.when(wanted & (j == 5))
            def _(load=load):
                for level, _, at, extra in places(True):
                    load(level, extra, at, near)

        @pl.when(phase == 1)
        def _():
            for level, row, at, _ in places():
                xs[at : at + 6, :] = x_ref[level, row, 16:24].astype(F32)[2:8]
                xs[at + 6 : at + 12, :] = from_right[level, row - 3].astype(F32)[0:6]

        @pl.when(phase == 2)
        def _():
            for level, row, at, _ in places():
                xs[at : at + 6, :] = from_left[level, row - 39].astype(F32)[2:8]

        lat_edge = ((j == 5) & (lat == n_lat - 1)).astype(jnp.int32)
        variants = [w // 4 + (2 * lat_edge if w % 2 else 0) for w in range(6)]
        attend(
            xs, qkv_ref, s_ref, p_ref, ctx_ref, bias_ref, variants,
            g1_ref, wqkv_ref, wk_ref, wp_ref, g2_ref, wup_ref, wdnt_ref,
        )

        @pl.when(inner)
        def _():
            for level, row, at, _ in places():
                o_ref[level, row, 6:18, :] = xs[at : at + 12, :].astype(BF)

        @pl.when(phase == 1)
        def _():
            for level, row, at, _ in places():
                o_ref[level, row, 18:24, :] = xs[at : at + 6, :].astype(BF)
                to_right[level, row - 3, 0:6, :] = xs[at + 6 : at + 12, :].astype(BF)

        @pl.when(phase == 2)
        def _():
            for level, row, at, _ in places():
                to_left[level, row - 39, 2:8, :] = xs[at : at + 6, :].astype(BF)
                o_ref[level, row, 0:6, :] = xs[at + 6 : at + 12, :].astype(BF)

        for n in range(3):
            @pl.when(s == 3 + n)
            def _(n=n):
                home_east[n].start()

            @pl.when(s == 6 + n)
            def _(n=n):
                home_west[2 - n].start()
                if n == 0:
                    home_diag.start()

        @pl.when(s == 9)
        def _():
            home_lat.start()

        return 0

    lax.fori_loop(0, 12, step, 0)
    for copy in home_east:
        copy.wait_recv()
    home_lat.wait_recv()
    home_diag.wait_recv()
    for copy in home_west:
        copy.wait_recv()

    def merge(level, _):
        for r in range(36):
            o_ref[level, 3 + r, 0:6, :] = back_left[level, r, 0:6, :]
        for r in range(33):
            o_ref[level, 39 + r, 18:24, :] = back_right[level, r, 2:8, :]
        for r in range(3):
            o_ref[level, r, 0:18, :] = back_lat[level, r, 0:18, :]
            o_ref[level, r, 18:24, :] = back_diag[level, r, 2:8, :]
        return 0

    lax.fori_loop(0, 6, merge, 0)
    for copy in (*halo, *home_east, *home_west, home_diag, home_lat):
        copy.wait_send()


def block(stream, position_bias, g1, wqkv, wp, g2, wup, wdn):
    vm = pl.BlockSpec(memory_space=pltpu.VMEM)
    slab = pltpu.VMEM((6, 36, 8, D), BF)
    out = pl.pallas_call(
        block_kernel,
        in_specs=[vm] * 8,
        out_specs=vm,
        out_shape=jax.ShapeDtypeStruct((6, 75, 24, D), BF),
        scratch_shapes=[
            pltpu.VMEM((6, 3, 24, D), BF),
            slab, slab, slab, slab,
            slab, pltpu.VMEM((6, 33, 8, D), BF),
            pltpu.VMEM((6, 3, 24, D), BF), pltpu.VMEM((6, 3, 8, D), BF),
            pltpu.VMEM((6 * WIN, D), F32),
            pltpu.VMEM((6 * WIN, 768), BF),
            pltpu.VMEM((2, HEADS * WIN, WIN), F32),
            pltpu.VMEM((2, HEADS * WIN, WIN), BF),
            pltpu.VMEM((6 * WIN, 256), BF),
            pltpu.VMEM((4, HEADS * WIN, WIN), F32),
            pltpu.VMEM((D, 256), BF),
            pltpu.SemaphoreType.DMA((12,)),
            pltpu.SemaphoreType.DMA((12,)),
        ],
        compiler_params=pltpu.CompilerParams(
            collective_id=0, has_side_effects=True, vmem_limit_bytes=32 << 20
        ),
    )(stream, position_bias.reshape(HEADS * WIN, WIN), g1.reshape(1, D), wqkv, wp, g2.reshape(1, D), wup, wdn.T)
    return out[:, :72]


def on_device(
    tokens,
    obs_values,
    obs_dest,
    obs_cell,
    obs_count,
    w_obs,
    ln1_gain,
    w_qkv,
    position_bias,
    w_proj,
    ln2_gain,
    w_up,
    w_down,
):
    received = ship(obs_dest, obs_cell, obs_count, obs_values, w_obs)
    stream = scatter(received, tokens)
    return block(stream, position_bias, ln1_gain, w_qkv, w_proj, ln2_gain, w_up, w_down)


def solution(mesh):
    in_specs = (
        P(None, "lat", "lon", None),
        P(("lon", "lat"), None),
        P(("lon", "lat")),
        P(("lon", "lat")),
        P(("lon", "lat")),
        P(),
        P(),
        P(),
        P(),
        P(),
        P(),
        P(),
        P(),
    )
    out_specs = P(None, "lat", "lon", None)
    return jax.shard_map(
        on_device, mesh=mesh, in_specs=in_specs, out_specs=out_specs, check_vma=False
    )
```

```python
import math

import jax
import jax.numpy as jnp
import numpy as np
from jax import lax
from jax.experimental import pallas as pl
from jax.experimental.pallas import tpu as pltpu
from jax.sharding import PartitionSpec as P

WZ = 2
WLAT = 6
WLON = 12
F32=jnp.float32; BF=jnp.bfloat16
WIN=144; D=192; HEADS=6; HD=32
NT=(((1,),(1,)),((),()))
LOG2E=math.log2(math.e)

def dot(a,b): return jnp.dot(a,b,preferred_element_type=F32)
def dot_nt(a,b): return lax.dot_general(a,b,NT,preferred_element_type=F32)

def norm(x, gain):
    mean=jnp.mean(x,axis=-1,keepdims=True)
    c=x-mean
    var=jnp.mean(c*c,axis=-1,keepdims=True)
    return (c*lax.rsqrt(var+1e-5)*gain).astype(BF)

def gelu(x):
    h=0.5*x
    return h+h*lax.erf(x*np.float32(math.sqrt(0.5)))

def head_mask(shape, h, width=HD):
    lane=lax.broadcasted_iota(jnp.int32,shape,len(shape)-1)
    return (lane>=h*width)&(lane<(h+1)*width)

GROUPS=((0,4,0),(4,2,128))
MESH=pl.DeviceIdType.MESH

def mask_rows(axis):
    at = lax.broadcasted_iota(jnp.int32, (WIN, WIN), axis)
    upper = at >= 72
    return upper, ((at >= 36) & (at < 72)) | (at >= 108)


def fill_bias(raw_ref, bias_ref):
    level_q, lat_q = mask_rows(0)
    level_k, lat_k = mask_rows(1)
    zero = jnp.zeros((WIN, WIN), F32)
    level_cut = jnp.where(level_q != level_k, -1e30, zero)
    lat_cut = jnp.where(lat_q != lat_k, -1e30, zero)
    both_cut = jnp.where((level_q != level_k) | (lat_q != lat_k), -1e30, zero)

    def head(h, _):
        rows = pl.ds(pl.multiple_of(h * WIN, WIN), WIN)
        b = raw_ref[rows, :] * np.float32(LOG2E)
        for v, cut in enumerate((zero, level_cut, lat_cut, both_cut)):
            bias_ref[v, rows, :] = b + cut
        return 0

    lax.fori_loop(0, HEADS, head, 0)


CAP = 32
DEV = 128
BLK = 56
CHUNK = 32
TN = (((0,), (0,)), ((), ()))


def ship_kernel(
    cnt_ref, dest_hbm, cell_hbm, val_hbm, wt_hbm, o_ref, y_ref, slot_ref, acc_ref, buf_ref,
    dest_ref, cell_ref, val_ref, wt_ref, send_sem, recv_sem, local_sem, load_sem,
):
    n_lat = lax.axis_size("lat")
    n = lax.axis_size("lon") * n_lat
    me = lax.axis_index("lon") * n_lat + lax.axis_index("lat")
    rows = val_ref.shape[0]

    def at(device):
        return (device // n_lat, lax.rem(device, n_lat))

    loads = [
        pltpu.make_async_copy(src, dst, load_sem.at[i])
        for i, (src, dst) in enumerate(
            ((val_hbm, val_ref), (wt_hbm, wt_ref), (cell_hbm, cell_ref), (dest_hbm, dest_ref))
        )
    ]
    for load in loads:
        load.start()
    barrier = pltpu.get_barrier_semaphore()

    def greet(i, _):
        pl.semaphore_signal(
            barrier, inc=1, device_id=at(lax.rem(me + i, n)), device_id_type=MESH
        )
        return 0

    lax.fori_loop(1, n, greet, 0)
    for load in loads:
        load.wait()

    eye = (
        lax.broadcasted_iota(jnp.int32, (8, 64), 0) == lax.broadcasted_iota(jnp.int32, (8, 64), 1)
    ).astype(BF)
    for c in range(0, rows, 512):
        y = dot_nt(val_ref[c : c + 512, :], wt_ref[...])
        cell = cell_ref[0:1, c : c + 512]
        ids = jnp.concatenate(
            [(cell >> 7).astype(F32), (cell & 127).astype(F32), jnp.zeros((6, 512), F32)], axis=0
        ).astype(BF)
        mark = lax.dot_general(ids, eye, TN, preferred_element_type=F32)
        y_ref[c : c + 512, 0:128] = y[:, 0:128].astype(BF)
        y_ref[c : c + 512, 128:256] = jnp.concatenate([y[:, 128:192], mark], axis=1).astype(BF)

    ahead = (
        lax.broadcasted_iota(jnp.int32, (256, 256), 0)
        < lax.broadcasted_iota(jnp.int32, (256, 256), 1)
    ).astype(F32).astype(BF)
    tile = lax.broadcasted_iota(jnp.int32, (DEV, 256), 0)
    carry = jnp.zeros((DEV, 1), F32)
    for c in range(0, rows, 256):
        dest = dest_ref[0:1, c : c + 256]
        live = lax.broadcasted_iota(jnp.int32, (1, 256), 1) + c < cnt_ref[0]
        away = dest - me + jnp.where(dest < me, n, 0)
        away = jnp.where(live, away, -1)
        match = (tile == away).astype(F32)
        before = dot(match.astype(BF), ahead) + carry
        rank = jnp.sum(match * before, axis=0, keepdims=True)
        carry = carry + jnp.sum(match, axis=1, keepdims=True)
        slot_ref[0:1, c : c + 256] = jnp.where(live, away * CAP + rank.astype(jnp.int32), -1)

    def copy_to(i):
        return pltpu.make_async_remote_copy(
            src_ref=buf_ref.at[i], dst_ref=o_ref.at[me],
            send_sem=send_sem.at[i], recv_sem=recv_sem.at[i],
            device_id=at(lax.rem(me + i, n)), device_id_type=MESH,
        )

    def copy_from(i):
        source = lax.rem(me + n - i, n)
        return pltpu.make_async_remote_copy(
            src_ref=buf_ref.at[i], dst_ref=o_ref.at[source],
            send_sem=send_sem.at[i], recv_sem=recv_sem.at[i],
            device_id=at(source), device_id_type=MESH,
        )

    lane = lax.broadcasted_iota(jnp.int32, (16, 128), 1)
    span = CHUNK * CAP
    index = lax.broadcasted_iota(jnp.int32, (span, 256), 0)

    def chunk(c, _):
        for b in range(0, rows, 256):
            hot = (index == slot_ref[0:1, b : b + 256] - c * span).astype(F32).astype(BF)
            part = dot(hot, y_ref[b : b + 256, :])
            if b == 0:
                acc_ref[...] = part
            else:
                acc_ref[...] += part

        def lay(i, _):
            r = pl.multiple_of(i * CAP, CAP)
            block = c * CHUNK + i
            buf_ref[block, 0:32, :] = acc_ref[pl.ds(r, 32), 0:128].astype(BF)
            rest = acc_ref[pl.ds(r, 32), 128:256]
            buf_ref[block, 32:48, :] = jnp.where(
                lane < 64, rest[0:16], pltpu.roll(rest[16:32], 64, 1)
            ).astype(BF)
            marks = jnp.zeros((8, 128), F32)
            for g in range(4):
                marks = jnp.where(
                    lane[:8] // 2 == g, pltpu.roll(rest[8 * g : 8 * g + 8], 64 + 2 * g, 1), marks
                )
            buf_ref[block, 48:56, :] = marks.astype(BF)
            return 0

        lax.fori_loop(0, CHUNK, lay, 0, unroll=4)

        @pl.when(c == 0)
        def _():
            pl.semaphore_wait(barrier, n - 1)

        def send(i, _):
            copy_to(c * CHUNK + i).start()
            return 0

        lax.fori_loop(jnp.where(c == 0, 1, 0), CHUNK, send, 0)
        return 0

    lax.fori_loop(0, DEV // CHUNK, chunk, 0)
    local = pltpu.make_async_copy(buf_ref.at[0], o_ref.at[me], local_sem)
    local.start()

    def land(i, _):
        copy_from(i).wait_recv()
        return 0

    lax.fori_loop(1, n, land, 0)

    def sent(i, _):
        copy_to(i).wait_send()
        return 0

    lax.fori_loop(1, n, sent, 0)
    local.wait()


def ship(obs_dest, obs_cell, obs_count, values, w_obs):
    rows = values.shape[0]
    sm = pl.BlockSpec(memory_space=pltpu.SMEM)
    vm = pl.BlockSpec(memory_space=pltpu.VMEM)
    hbm = pl.BlockSpec(memory_space=pltpu.HBM)
    return pl.pallas_call(
        ship_kernel,
        in_specs=[sm, hbm, hbm, hbm, hbm],
        out_specs=vm,
        out_shape=jax.ShapeDtypeStruct((DEV, BLK, 128), BF),
        scratch_shapes=[
            pltpu.VMEM((rows, 256), BF),
            pltpu.VMEM((1, rows), jnp.int32),
            pltpu.VMEM((CHUNK * CAP, 256), F32),
            pltpu.VMEM((DEV, BLK, 128), BF),
            pltpu.VMEM((1, rows), jnp.int32),
            pltpu.VMEM((1, rows), jnp.int32),
            pltpu.VMEM(values.shape, BF),
            pltpu.VMEM((D, values.shape[1]), BF),
            pltpu.SemaphoreType.DMA((DEV,)),
            pltpu.SemaphoreType.DMA((DEV,)),
            pltpu.SemaphoreType.DMA,
            pltpu.SemaphoreType.DMA((4,)),
        ],
        compiler_params=pltpu.CompilerParams(
            collective_id=1, has_side_effects=True, vmem_limit_bytes=20 << 20
        ),
    )(obs_count, obs_dest.reshape(1, rows), obs_cell.reshape(1, rows), values, w_obs.T)


def scatter_kernel(recv_ref, tok_hbm, out_ref, tok_ref, tok_sem, rows, ids_v, ids_s, sem, *accs):
    fetch = pltpu.make_async_copy(tok_hbm, tok_ref, tok_sem)
    fetch.start()
    cells = tok_ref.shape[0]
    group = lax.broadcasted_iota(jnp.int32, (8, 128), 0)
    lane = lax.broadcasted_iota(jnp.int32, (8, 128), 1)
    sel = jnp.where(lane == 2 * group, 128.0, jnp.where(lane == 2 * group + 1, 1.0, 0.0)).astype(BF)
    for b in range(8):
        marks = recv_ref[16 * b : 16 * b + 16, 48:56, :].astype(F32).reshape(128, 128).astype(BF)
        ids_v[:, 128 * b : 128 * b + 128] = 2 * (dot_nt(sel, marks) + 0.5).astype(jnp.int32)
    cp = pltpu.make_async_copy(ids_v, ids_s, sem)
    cp.start()

    def prep(d, _):
        r = pl.multiple_of(d * 64, 64)
        rows[pl.ds(r, 32, stride=2), :] = recv_ref[d, 0:32, :].astype(F32)
        rest = recv_ref[d, 32:48, :].astype(F32)
        rows[pl.ds(r + 1, 16, stride=2), :] = rest
        rows[pl.ds(r + 33, 16, stride=2), :] = pltpu.roll(rest, 64, 1)
        return 0

    lax.fori_loop(0, DEV, prep, 0, unroll=4)
    for acc in accs[1:]:

        def clear(g, _, acc=acc):
            acc[pl.ds(pl.multiple_of(g * 288, 288), 288), :] = jnp.zeros((288, 128), F32)
            return 0

        lax.fori_loop(0, cells // 144, clear, 0)
    fetch.wait()

    def init(g, _):
        r = pl.multiple_of(g * 144, 144)
        t = tok_ref[pl.ds(r, 144), :].astype(F32)
        accs[0][pl.ds(2 * r, 144, stride=2), :] = t[:, 0:128]
        accs[0][pl.ds(2 * r + 1, 144, stride=2), 0:64] = t[:, 128:192]
        return 0

    lax.fori_loop(0, cells // 144, init, 0)
    cp.wait()
    half = DEV // len(accs)

    def body(d, _):
        for j in range(0, CAP, 2):
            for a, acc in enumerate(accs):
                src = d + a * half
                first = ids_s[j // 8, src * 8 + j % 8]
                second = ids_s[(j + 1) // 8, src * 8 + (j + 1) % 8]
                row = 2 * (src * CAP + j)
                old = acc[pl.ds(second, 2), :]
                new = acc[pl.ds(first, 2), :] + rows[pl.ds(row, 2), :]
                old = jnp.where(first == second, new, old)
                acc[pl.ds(first, 2), :] = new
                acc[pl.ds(second, 2), :] = old + rows[pl.ds(row + 2, 2), :]
        return 0

    lax.fori_loop(0, half, body, 0)

    def fin(g, _):
        r = pl.multiple_of(g * 144, 144)
        t = accs[0][pl.ds(2 * r, 144, stride=2), :]
        for a in accs[1:]:
            t = t + a[pl.ds(2 * r, 144, stride=2), :]
        out_ref[pl.ds(r, 144), 0:128] = t.astype(BF)
        t = accs[0][pl.ds(2 * r + 1, 144, stride=2), :]
        for a in accs[1:]:
            t = t + a[pl.ds(2 * r + 1, 144, stride=2), :]
        out_ref[pl.ds(r, 144), 128:192] = t[:, 0:64].astype(BF)
        return 0

    lax.fori_loop(0, cells // 144, fin, 0)


def scatter(recv, tokens):
    cells = 6 * 72 * 24
    vm = pl.BlockSpec(memory_space=pltpu.VMEM)
    out = pl.pallas_call(
        scatter_kernel,
        in_specs=[vm, pl.BlockSpec(memory_space=pltpu.HBM)],
        out_specs=vm,
        out_shape=jax.ShapeDtypeStruct((cells, D), BF),
        scratch_shapes=[
            pltpu.VMEM((cells, D), BF),
            pltpu.SemaphoreType.DMA,
            pltpu.VMEM((2 * DEV * CAP, 128), F32),
            pltpu.VMEM((8, 1024), jnp.int32),
            pltpu.SMEM((8, 1024), jnp.int32),
            pltpu.SemaphoreType.DMA,
            pltpu.VMEM((2 * cells, 128), F32),
            pltpu.VMEM((2 * cells, 128), F32),
        ],
        compiler_params=pltpu.CompilerParams(vmem_limit_bytes=36 << 20),
    )(recv, tokens.reshape(cells, D))
    return out.reshape(tokens.shape)


def attend(xs, qkv_ref, s_ref, p_ref, ctx_ref, bias_ref, variants, g1_ref, wqkv_ref, wk_ref, wp_ref, g2_ref, wup_ref, wdnt_ref):
    zero = jnp.zeros((), BF)
    count = len(variants)
    n1 = norm(xs[...], g1_ref[...])
    qkv_ref[:, 0:256] = (
        dot(n1, wqkv_ref[:, 0:256]) * np.float32(LOG2E / math.sqrt(HD))
    ).astype(BF)
    qkv_ref[:, 256:512] = dot(n1, wk_ref[...]).astype(BF)
    qkv_ref[:, 512:704] = dot(n1, wqkv_ref[:, 384:576]).astype(BF)

    def scores(w):
        sl = slice(w * WIN, (w + 1) * WIN)
        for h0, nh, l0 in GROUPS:
            qg = qkv_ref[sl, l0 : l0 + 128]
            kg = qkv_ref[sl, 256 + l0 : 384 + l0]
            qs = jnp.concatenate(
                [jnp.where(head_mask((WIN, 128), h), qg, zero) for h in range(nh)], axis=0
            )
            s_ref[w % 2, h0 * WIN : (h0 + nh) * WIN, :] = dot_nt(qs, kg)

    def softmax(w):
        sl = slice(w * WIN, (w + 1) * WIN)
        sums = []
        for h in range(HEADS):
            rows = slice(h * WIN, (h + 1) * WIN)
            s = s_ref[w % 2, rows, :] + bias_ref[variants[w], rows, :]
            p = jnp.exp2(s - jnp.max(s, axis=-1, keepdims=True))
            sums.append(jnp.sum(p, axis=-1, keepdims=True))
            p_ref[w % 2, rows, :] = p.astype(BF)
        for h0, nh, l0 in GROUPS:
            o = dot(p_ref[w % 2, h0 * WIN : (h0 + nh) * WIN, :], qkv_ref[sl, 512 + l0 : 640 + l0])
            c = o[:WIN]
            total = sums[h0] * jnp.ones((1, 128), F32)
            for h in range(1, nh):
                mask = head_mask((WIN, 128), h)
                c = jnp.where(mask, o[h * WIN : (h + 1) * WIN], c)
                total = jnp.where(mask, sums[h0 + h], total)
            ctx_ref[sl, l0 : l0 + 128] = (c * (1.0 / total)).astype(BF)

    scores(0)
    for w in range(count):
        if w + 1 < count:
            scores(w + 1)
        softmax(w)
    att = (xs[...] + dot(ctx_ref[:, :D], wp_ref[...])).astype(BF).astype(F32)
    n2 = norm(att, g2_ref[...])
    acc = att
    for j in range(3):
        hid = gelu(dot(n2, wup_ref[:, j * 256 : (j + 1) * 256])).astype(BF)
        acc = acc + dot_nt(hid, wdnt_ref[:, j * 256 : (j + 1) * 256])
    xs[...] = acc


def block_kernel(
    x_ref, raw_ref, g1_ref, wqkv_ref, wp_ref, g2_ref, wup_ref, wdnt_ref, o_ref,
    near, from_right, from_left, to_right, to_left, back_left, back_right, back_lat, back_diag,
    xs, qkv_ref, s_ref, p_ref, ctx_ref, bias_ref, wk_ref, send_sem, recv_sem,
):
    lon = lax.axis_index("lon")
    lat = lax.axis_index("lat")
    n_lon = lax.axis_size("lon")
    n_lat = lax.axis_size("lat")
    east = lax.rem(lon + 1, n_lon)
    west = lax.rem(lon + n_lon - 1, n_lon)
    north = lax.rem(lat + 1, n_lat)
    south = lax.rem(lat + n_lat - 1, n_lat)

    barrier = pltpu.get_barrier_semaphore()
    partners = ((east, lat), (west, lat), (lon, north), (lon, south), (east, south), (west, north))
    for partner in partners:
        pl.semaphore_signal(barrier, inc=1, device_id=partner, device_id_type=MESH)
    fill_bias(raw_ref, bias_ref)
    wk_ref[...] = pltpu.roll(wqkv_ref[:, 128:384].astype(F32), 192, 1).astype(BF)
    qkv_ref[:, 704:768] = jnp.zeros((6 * WIN, 64), BF)
    pl.semaphore_wait(barrier, len(partners))

    def remote(n, src, dst, target):
        return pltpu.make_async_remote_copy(
            src_ref=src, dst_ref=dst, send_sem=send_sem.at[n], recv_sem=recv_sem.at[n],
            device_id=target, device_id_type=MESH,
        )

    halo = [
        remote(0, x_ref.at[:, 3:39, 0:8], from_right, (west, lat)),
        remote(1, x_ref.at[:, 39:72, 16:24], from_left.at[:, 0:33], (east, lat)),
        remote(2, x_ref.at[:, 0:3], near, (lon, south)),
        remote(3, x_ref.at[:, 0:3, 16:24], from_left.at[:, 33:36], (east, south)),
    ]
    home_east = [
        remote(4 + j, to_right.at[:, 12 * j : 12 * j + 12], back_left.at[:, 12 * j : 12 * j + 12], (east, lat))
        for j in range(3)
    ]
    home_west = [
        remote(7 + j, to_left.at[:, 12 * j : end], back_right.at[:, 12 * j : end], (west, lat))
        for j, end in enumerate((12, 24, 33))
    ]
    home_diag = remote(10, to_left.at[:, 33:36], back_diag, (west, north))
    home_lat = remote(11, o_ref.at[:, 72:75], back_lat, (lon, north))
    for copy in halo:
        copy.start()

    def step(s, _):
        phase = s // 3
        turn = lax.rem(s, 3)
        j = jnp.where(phase < 2, turn, 5 - turn)
        inner = (phase == 0) | (phase == 3)

        @pl.when(s == 3)
        def _():
            halo[0].wait_recv()

        @pl.when(s == 6)
        def _():
            for copy in halo[1:]:
                copy.wait_recv()

        def places(last=None):
            for w in range(6):
                for i in range(2):
                    for r in range(6):
                        if last is not None and last != (w % 2 == 1 and r >= 3):
                            continue
                        level = (w // 2 * 2 + 1 + i) % 6
                        row = 3 + 6 * (2 * j + w % 2) + r
                        yield level, row, w * WIN + (i * 6 + r) * 12, r - 3

        def load_inner(level, row, at, source):
            xs[at : at + 12, :] = source[level, row].astype(F32)[6:18]

        def load_left(level, row, at, source):
            xs[at + 6 : at + 12, :] = source[level, row, 0:8].astype(F32)[0:6]

        for wanted, load in ((inner, load_inner), (phase == 2, load_left)):
            @pl.when(wanted)
            def _(load=load):
                for level, row, at, _ in places(False):
                    load(level, row, at, x_ref)

            @pl.when(wanted & (j < 5))
            def _(load=load):
                for level, row, at, _ in places(True):
                    load(level, row, at, x_ref)

            @pl.when(wanted & (j == 5))
            def _(load=load):
                for level, _, at, extra in places(True):
                    load(level, extra, at, near)

        @pl.when(phase == 1)
        def _():
            for level, row, at, _ in places():
                xs[at : at + 6, :] = x_ref[level, row, 16:24].astype(F32)[2:8]
                xs[at + 6 : at + 12, :] = from_right[level, row - 3].astype(F32)[0:6]

        @pl.when(phase == 2)
        def _():
            for level, row, at, _ in places():
                xs[at : at + 6, :] = from_left[level, row - 39].astype(F32)[2:8]

        lat_edge = ((j == 5) & (lat == n_lat - 1)).astype(jnp.int32)
        variants = [w // 4 + (2 * lat_edge if w % 2 else 0) for w in range(6)]
        attend(
            xs, qkv_ref, s_ref, p_ref, ctx_ref, bias_ref, variants,
            g1_ref, wqkv_ref, wk_ref, wp_ref, g2_ref, wup_ref, wdnt_ref,
        )

        @pl.when(inner)
        def _():
            for level, row, at, _ in places():
                o_ref[level, row, 6:18, :] = xs[at : at + 12, :].astype(BF)

        @pl.when(phase == 1)
        def _():
            for level, row, at, _ in places():
                o_ref[level, row, 18:24, :] = xs[at : at + 6, :].astype(BF)
                to_right[level, row - 3, 0:6, :] = xs[at + 6 : at + 12, :].astype(BF)

        @pl.when(phase == 2)
        def _():
            for level, row, at, _ in places():
                to_left[level, row - 39, 2:8, :] = xs[at : at + 6, :].astype(BF)
                o_ref[level, row, 0:6, :] = xs[at + 6 : at + 12, :].astype(BF)

        for n in range(3):
            @pl.when(s == 3 + n)
            def _(n=n):
                home_east[n].start()

            @pl.when(s == 6 + n)
            def _(n=n):
                home_west[2 - n].start()
                if n == 0:
                    home_diag.start()

        @pl.when(s == 9)
        def _():
            home_lat.start()

        return 0

    lax.fori_loop(0, 12, step, 0)
    for copy in home_east:
        copy.wait_recv()
    home_lat.wait_recv()
    home_diag.wait_recv()
    for copy in home_west:
        copy.wait_recv()

    def merge(level, _):
        for r in range(36):
            o_ref[level, 3 + r, 0:6, :] = back_left[level, r, 0:6, :]
        for r in range(33):
            o_ref[level, 39 + r, 18:24, :] = back_right[level, r, 2:8, :]
        for r in range(3):
            o_ref[level, r, 0:18, :] = back_lat[level, r, 0:18, :]
            o_ref[level, r, 18:24, :] = back_diag[level, r, 2:8, :]
        return 0

    lax.fori_loop(0, 6, merge, 0)
    for copy in (*halo, *home_east, *home_west, home_diag, home_lat):
        copy.wait_send()


def block(stream, position_bias, g1, wqkv, wp, g2, wup, wdn):
    vm = pl.BlockSpec(memory_space=pltpu.VMEM)
    slab = pltpu.VMEM((6, 36, 8, D), BF)
    out = pl.pallas_call(
        block_kernel,
        in_specs=[vm] * 8,
        out_specs=vm,
        out_shape=jax.ShapeDtypeStruct((6, 75, 24, D), BF),
        scratch_shapes=[
            pltpu.VMEM((6, 3, 24, D), BF),
            slab, slab, slab, slab,
            slab, pltpu.VMEM((6, 33, 8, D), BF),
            pltpu.VMEM((6, 3, 24, D), BF), pltpu.VMEM((6, 3, 8, D), BF),
            pltpu.VMEM((6 * WIN, D), F32),
            pltpu.VMEM((6 * WIN, 768), BF),
            pltpu.VMEM((2, HEADS * WIN, WIN), F32),
            pltpu.VMEM((2, HEADS * WIN, WIN), BF),
            pltpu.VMEM((6 * WIN, 256), BF),
            pltpu.VMEM((4, HEADS * WIN, WIN), F32),
            pltpu.VMEM((D, 256), BF),
            pltpu.SemaphoreType.DMA((12,)),
            pltpu.SemaphoreType.DMA((12,)),
        ],
        compiler_params=pltpu.CompilerParams(
            collective_id=0, has_side_effects=True, vmem_limit_bytes=32 << 20
        ),
    )(stream, position_bias.reshape(HEADS * WIN, WIN), g1.reshape(1, D), wqkv, wp, g2.reshape(1, D), wup, wdn.T)
    return out[:, :72]


def on_device(
    tokens,
    obs_values,
    obs_dest,
    obs_cell,
    obs_count,
    w_obs,
    ln1_gain,
    w_qkv,
    position_bias,
    w_proj,
    ln2_gain,
    w_up,
    w_down,
):
    received = ship(obs_dest, obs_cell, obs_count, obs_values, w_obs)
    stream = scatter(received, tokens)
    return block(stream, position_bias, ln1_gain, w_qkv, w_proj, ln2_gain, w_up, w_down)


def solution(mesh):
    in_specs = (
        P(None, "lat", "lon", None),
        P(("lon", "lat"), None),
        P(("lon", "lat")),
        P(("lon", "lat")),
        P(("lon", "lat")),
        P(),
        P(),
        P(),
        P(),
        P(),
        P(),
        P(),
        P(),
    )
    out_specs = P(None, "lat", "lon", None)
    return jax.shard_map(
        on_device, mesh=mesh, in_specs=in_specs, out_specs=out_specs, check_vma=False
    )
```

```python
import math

import jax
import jax.numpy as jnp
import numpy as np
from jax import lax
from jax.experimental import pallas as pl
from jax.experimental.pallas import tpu as pltpu
from jax.sharding import PartitionSpec as P

WZ = 2
WLAT = 6
WLON = 12
F32=jnp.float32; BF=jnp.bfloat16
WIN=144; D=192; HEADS=6; HD=32
NT=(((1,),(1,)),((),()))
LOG2E=math.log2(math.e)

def dot(a,b): return jnp.dot(a,b,preferred_element_type=F32)
def dot_nt(a,b): return lax.dot_general(a,b,NT,preferred_element_type=F32)

def norm(x, gain):
    mean=jnp.mean(x,axis=-1,keepdims=True)
    c=x-mean
    var=jnp.mean(c*c,axis=-1,keepdims=True)
    return (c*lax.rsqrt(var+1e-5)*gain).astype(BF)

def gelu(x):
    h=0.5*x
    return h+h*lax.erf(x*np.float32(math.sqrt(0.5)))

def head_mask(shape, h, width=HD):
    lane=lax.broadcasted_iota(jnp.int32,shape,len(shape)-1)
    return (lane>=h*width)&(lane<(h+1)*width)

GROUPS=((0,4,0),(4,2,128))
MESH=pl.DeviceIdType.MESH

def mask_rows(axis):
    at = lax.broadcasted_iota(jnp.int32, (WIN, WIN), axis)
    upper = at >= 72
    return upper, ((at >= 36) & (at < 72)) | (at >= 108)


def fill_bias(raw_ref, bias_ref):
    level_q, lat_q = mask_rows(0)
    level_k, lat_k = mask_rows(1)
    zero = jnp.zeros((WIN, WIN), F32)
    level_cut = jnp.where(level_q != level_k, -1e30, zero)
    lat_cut = jnp.where(lat_q != lat_k, -1e30, zero)
    both_cut = jnp.where((level_q != level_k) | (lat_q != lat_k), -1e30, zero)

    def head(h, _):
        rows = pl.ds(pl.multiple_of(h * WIN, WIN), WIN)
        b = raw_ref[rows, :] * np.float32(LOG2E)
        for v, cut in enumerate((zero, level_cut, lat_cut, both_cut)):
            bias_ref[v, rows, :] = b + cut
        return 0

    lax.fori_loop(0, HEADS, head, 0)


CAP = 32
DEV = 128
BLK = 56
CHUNK = 32
TN = (((0,), (0,)), ((), ()))


def ship_kernel(
    cnt_ref, dest_hbm, cell_hbm, val_hbm, wt_hbm, o_ref, y_ref, slot_ref, acc_ref, buf_ref,
    dest_ref, cell_ref, val_ref, wt_ref, send_sem, recv_sem, local_sem, load_sem,
):
    n_lat = lax.axis_size("lat")
    n = lax.axis_size("lon") * n_lat
    me = lax.axis_index("lon") * n_lat + lax.axis_index("lat")
    rows = val_ref.shape[0]

    def at(device):
        return (device // n_lat, lax.rem(device, n_lat))

    loads = [
        pltpu.make_async_copy(src, dst, load_sem.at[i])
        for i, (src, dst) in enumerate(
            ((val_hbm, val_ref), (wt_hbm, wt_ref), (cell_hbm, cell_ref), (dest_hbm, dest_ref))
        )
    ]
    for load in loads:
        load.start()
    barrier = pltpu.get_barrier_semaphore()

    def greet(i, _):
        pl.semaphore_signal(
            barrier, inc=1, device_id=at(lax.rem(me + i, n)), device_id_type=MESH
        )
        return 0

    lax.fori_loop(1, n, greet, 0)
    for load in loads:
        load.wait()

    eye = (
        lax.broadcasted_iota(jnp.int32, (8, 64), 0) == lax.broadcasted_iota(jnp.int32, (8, 64), 1)
    ).astype(BF)
    for c in range(0, rows, 512):
        y = dot_nt(val_ref[c : c + 512, :], wt_ref[...])
        cell = cell_ref[0:1, c : c + 512]
        ids = jnp.concatenate(
            [(cell >> 7).astype(F32), (cell & 127).astype(F32), jnp.zeros((6, 512), F32)], axis=0
        ).astype(BF)
        mark = lax.dot_general(ids, eye, TN, preferred_element_type=F32)
        y_ref[c : c + 512, 0:128] = y[:, 0:128].astype(BF)
        y_ref[c : c + 512, 128:256] = jnp.concatenate([y[:, 128:192], mark], axis=1).astype(BF)

    ahead = (
        lax.broadcasted_iota(jnp.int32, (256, 256), 0)
        < lax.broadcasted_iota(jnp.int32, (256, 256), 1)
    ).astype(F32).astype(BF)
    tile = lax.broadcasted_iota(jnp.int32, (DEV, 256), 0)
    carry = jnp.zeros((DEV, 1), F32)
    for c in range(0, rows, 256):
        dest = dest_ref[0:1, c : c + 256]
        live = lax.broadcasted_iota(jnp.int32, (1, 256), 1) + c < cnt_ref[0]
        away = dest - me + jnp.where(dest < me, n, 0)
        away = jnp.where(live, away, -1)
        match = (tile == away).astype(F32)
        before = dot(match.astype(BF), ahead) + carry
        rank = jnp.sum(match * before, axis=0, keepdims=True)
        carry = carry + jnp.sum(match, axis=1, keepdims=True)
        slot_ref[0:1, c : c + 256] = jnp.where(live, away * CAP + rank.astype(jnp.int32), -1)

    def copy_to(i):
        return pltpu.make_async_remote_copy(
            src_ref=buf_ref.at[i], dst_ref=o_ref.at[me],
            send_sem=send_sem.at[i], recv_sem=recv_sem.at[i],
            device_id=at(lax.rem(me + i, n)), device_id_type=MESH,
        )

    def copy_from(i):
        source = lax.rem(me + n - i, n)
        return pltpu.make_async_remote_copy(
            src_ref=buf_ref.at[i], dst_ref=o_ref.at[source],
            send_sem=send_sem.at[i], recv_sem=recv_sem.at[i],
            device_id=at(source), device_id_type=MESH,
        )

    lane = lax.broadcasted_iota(jnp.int32, (16, 128), 1)
    span = CHUNK * CAP
    index = lax.broadcasted_iota(jnp.int32, (span, 256), 0)

    def chunk(c, _):
        for b in range(0, rows, 256):
            hot = (index == slot_ref[0:1, b : b + 256] - c * span).astype(F32).astype(BF)
            part = dot(hot, y_ref[b : b + 256, :])
            if b == 0:
                acc_ref[...] = part
            else:
                acc_ref[...] += part

        def lay(i, _):
            r = pl.multiple_of(i * CAP, CAP)
            block = c * CHUNK + i
            buf_ref[block, 0:32, :] = acc_ref[pl.ds(r, 32), 0:128].astype(BF)
            rest = acc_ref[pl.ds(r, 32), 128:256]
            buf_ref[block, 32:48, :] = jnp.where(
                lane < 64, rest[0:16], pltpu.roll(rest[16:32], 64, 1)
            ).astype(BF)
            marks = jnp.zeros((8, 128), F32)
            for g in range(4):
                marks = jnp.where(
                    lane[:8] // 2 == g, pltpu.roll(rest[8 * g : 8 * g + 8], 64 + 2 * g, 1), marks
                )
            buf_ref[block, 48:56, :] = marks.astype(BF)
            return 0

        lax.fori_loop(0, CHUNK, lay, 0, unroll=4)

        @pl.when(c == 0)
        def _():
            pl.semaphore_wait(barrier, n - 1)

        def send(i, _):
            copy_to(c * CHUNK + i).start()
            return 0

        lax.fori_loop(jnp.where(c == 0, 1, 0), CHUNK, send, 0)
        return 0

    lax.fori_loop(0, DEV // CHUNK, chunk, 0)
    local = pltpu.make_async_copy(buf_ref.at[0], o_ref.at[me], local_sem)
    local.start()

    def land(i, _):
        copy_from(i).wait_recv()
        return 0

    lax.fori_loop(1, n, land, 0)

    def sent(i, _):
        copy_to(i).wait_send()
        return 0

    lax.fori_loop(1, n, sent, 0)
    local.wait()


def ship(obs_dest, obs_cell, obs_count, values, w_obs):
    rows = values.shape[0]
    sm = pl.BlockSpec(memory_space=pltpu.SMEM)
    vm = pl.BlockSpec(memory_space=pltpu.VMEM)
    hbm = pl.BlockSpec(memory_space=pltpu.HBM)
    return pl.pallas_call(
        ship_kernel,
        in_specs=[sm, hbm, hbm, hbm, hbm],
        out_specs=vm,
        out_shape=jax.ShapeDtypeStruct((DEV, BLK, 128), BF),
        scratch_shapes=[
            pltpu.VMEM((rows, 256), BF),
            pltpu.VMEM((1, rows), jnp.int32),
            pltpu.VMEM((CHUNK * CAP, 256), F32),
            pltpu.VMEM((DEV, BLK, 128), BF),
            pltpu.VMEM((1, rows), jnp.int32),
            pltpu.VMEM((1, rows), jnp.int32),
            pltpu.VMEM(values.shape, BF),
            pltpu.VMEM((D, values.shape[1]), BF),
            pltpu.SemaphoreType.DMA((DEV,)),
            pltpu.SemaphoreType.DMA((DEV,)),
            pltpu.SemaphoreType.DMA,
            pltpu.SemaphoreType.DMA((4,)),
        ],
        compiler_params=pltpu.CompilerParams(
            collective_id=1, has_side_effects=True, vmem_limit_bytes=62_000_000
        ),
    )(obs_count, obs_dest.reshape(1, rows), obs_cell.reshape(1, rows), values, w_obs.T)


def scatter_kernel(recv_ref, tok_hbm, out_ref, tok_ref, tok_sem, rows, ids_v, ids_s, sem, *accs):
    fetch = pltpu.make_async_copy(tok_hbm, tok_ref, tok_sem)
    fetch.start()
    cells = tok_ref.shape[0]
    group = lax.broadcasted_iota(jnp.int32, (8, 128), 0)
    lane = lax.broadcasted_iota(jnp.int32, (8, 128), 1)
    sel = jnp.where(lane == 2 * group, 128.0, jnp.where(lane == 2 * group + 1, 1.0, 0.0)).astype(BF)
    for b in range(8):
        marks = recv_ref[16 * b : 16 * b + 16, 48:56, :].astype(F32).reshape(128, 128).astype(BF)
        ids_v[:, 128 * b : 128 * b + 128] = 2 * (dot_nt(sel, marks) + 0.5).astype(jnp.int32)
    cp = pltpu.make_async_copy(ids_v, ids_s, sem)
    cp.start()

    def prep(d, _):
        r = pl.multiple_of(d * 64, 64)
        rows[pl.ds(r, 32, stride=2), :] = recv_ref[d, 0:32, :].astype(F32)
        rest = recv_ref[d, 32:48, :].astype(F32)
        rows[pl.ds(r + 1, 16, stride=2), :] = rest
        rows[pl.ds(r + 33, 16, stride=2), :] = pltpu.roll(rest, 64, 1)
        return 0

    lax.fori_loop(0, DEV, prep, 0, unroll=4)
    for acc in accs[1:]:

        def clear(g, _, acc=acc):
            acc[pl.ds(pl.multiple_of(g * 288, 288), 288), :] = jnp.zeros((288, 128), F32)
            return 0

        lax.fori_loop(0, cells // 144, clear, 0)
    fetch.wait()

    def init(g, _):
        r = pl.multiple_of(g * 144, 144)
        t = tok_ref[pl.ds(r, 144), :].astype(F32)
        accs[0][pl.ds(2 * r, 144, stride=2), :] = t[:, 0:128]
        accs[0][pl.ds(2 * r + 1, 144, stride=2), 0:64] = t[:, 128:192]
        return 0

    lax.fori_loop(0, cells // 144, init, 0)
    cp.wait()
    half = DEV // len(accs)

    def body(d, _):
        for j in range(0, CAP, 2):
            for a, acc in enumerate(accs):
                src = d + a * half
                first = ids_s[j // 8, src * 8 + j % 8]
                second = ids_s[(j + 1) // 8, src * 8 + (j + 1) % 8]
                row = 2 * (src * CAP + j)
                old = acc[pl.ds(second, 2), :]
                new = acc[pl.ds(first, 2), :] + rows[pl.ds(row, 2), :]
                old = jnp.where(first == second, new, old)
                acc[pl.ds(first, 2), :] = new
                acc[pl.ds(second, 2), :] = old + rows[pl.ds(row + 2, 2), :]
        return 0

    lax.fori_loop(0, half, body, 0)

    def fin(g, _):
        r = pl.multiple_of(g * 144, 144)
        t = accs[0][pl.ds(2 * r, 144, stride=2), :]
        for a in accs[1:]:
            t = t + a[pl.ds(2 * r, 144, stride=2), :]
        out_ref[pl.ds(r, 144), 0:128] = t.astype(BF)
        t = accs[0][pl.ds(2 * r + 1, 144, stride=2), :]
        for a in accs[1:]:
            t = t + a[pl.ds(2 * r + 1, 144, stride=2), :]
        out_ref[pl.ds(r, 144), 128:192] = t[:, 0:64].astype(BF)
        return 0

    lax.fori_loop(0, cells // 144, fin, 0)


def scatter(recv, tokens):
    cells = 6 * 72 * 24
    vm = pl.BlockSpec(memory_space=pltpu.VMEM)
    out = pl.pallas_call(
        scatter_kernel,
        in_specs=[vm, pl.BlockSpec(memory_space=pltpu.HBM)],
        out_specs=vm,
        out_shape=jax.ShapeDtypeStruct((cells, D), BF),
        scratch_shapes=[
            pltpu.VMEM((cells, D), BF),
            pltpu.SemaphoreType.DMA,
            pltpu.VMEM((2 * DEV * CAP, 128), F32),
            pltpu.VMEM((8, 1024), jnp.int32),
            pltpu.SMEM((8, 1024), jnp.int32),
            pltpu.SemaphoreType.DMA,
            pltpu.VMEM((2 * cells, 128), F32),
            pltpu.VMEM((2 * cells, 128), F32),
        ],
        compiler_params=pltpu.CompilerParams(vmem_limit_bytes=36 << 20),
    )(recv, tokens.reshape(cells, D))
    return out.reshape(tokens.shape)


def attend(xs, qkv_ref, s_ref, p_ref, ctx_ref, bias_ref, variants, g1_ref, wqkv_ref, wk_ref, wp_ref, g2_ref, wup_ref, wdnt_ref):
    zero = jnp.zeros((), BF)
    count = len(variants)
    n1 = norm(xs[...], g1_ref[...])
    qkv_ref[:, 0:256] = (
        dot(n1, wqkv_ref[:, 0:256]) * np.float32(LOG2E / math.sqrt(HD))
    ).astype(BF)
    qkv_ref[:, 256:512] = dot(n1, wk_ref[...]).astype(BF)
    qkv_ref[:, 512:704] = dot(n1, wqkv_ref[:, 384:576]).astype(BF)

    def scores(w):
        sl = slice(w * WIN, (w + 1) * WIN)
        for h0, nh, l0 in GROUPS:
            qg = qkv_ref[sl, l0 : l0 + 128]
            kg = qkv_ref[sl, 256 + l0 : 384 + l0]
            qs = jnp.concatenate(
                [jnp.where(head_mask((WIN, 128), h), qg, zero) for h in range(nh)], axis=0
            )
            s_ref[w % 2, h0 * WIN : (h0 + nh) * WIN, :] = dot_nt(qs, kg)

    def softmax(w):
        sl = slice(w * WIN, (w + 1) * WIN)
        sums = []
        for h in range(HEADS):
            rows = slice(h * WIN, (h + 1) * WIN)
            s = s_ref[w % 2, rows, :] + bias_ref[variants[w], rows, :]
            p = jnp.exp2(s - jnp.max(s, axis=-1, keepdims=True))
            sums.append(jnp.sum(p, axis=-1, keepdims=True))
            p_ref[w % 2, rows, :] = p.astype(BF)
        for h0, nh, l0 in GROUPS:
            o = dot(p_ref[w % 2, h0 * WIN : (h0 + nh) * WIN, :], qkv_ref[sl, 512 + l0 : 640 + l0])
            c = o[:WIN]
            total = sums[h0] * jnp.ones((1, 128), F32)
            for h in range(1, nh):
                mask = head_mask((WIN, 128), h)
                c = jnp.where(mask, o[h * WIN : (h + 1) * WIN], c)
                total = jnp.where(mask, sums[h0 + h], total)
            ctx_ref[sl, l0 : l0 + 128] = (c * (1.0 / total)).astype(BF)

    scores(0)
    for w in range(count):
        if w + 1 < count:
            scores(w + 1)
        softmax(w)
    att = (xs[...] + dot(ctx_ref[:, :D], wp_ref[...])).astype(BF).astype(F32)
    n2 = norm(att, g2_ref[...])
    acc = att
    for j in range(3):
        hid = gelu(dot(n2, wup_ref[:, j * 256 : (j + 1) * 256])).astype(BF)
        acc = acc + dot_nt(hid, wdnt_ref[:, j * 256 : (j + 1) * 256])
    xs[...] = acc


def block_kernel(
    x_ref, raw_ref, g1_ref, wqkv_ref, wp_ref, g2_ref, wup_ref, wdnt_ref, o_ref,
    near, from_right, from_left, to_right, to_left, back_left, back_right, back_lat, back_diag,
    xs, qkv_ref, s_ref, p_ref, ctx_ref, bias_ref, wk_ref, send_sem, recv_sem,
):
    lon = lax.axis_index("lon")
    lat = lax.axis_index("lat")
    n_lon = lax.axis_size("lon")
    n_lat = lax.axis_size("lat")
    east = lax.rem(lon + 1, n_lon)
    west = lax.rem(lon + n_lon - 1, n_lon)
    north = lax.rem(lat + 1, n_lat)
    south = lax.rem(lat + n_lat - 1, n_lat)

    barrier = pltpu.get_barrier_semaphore()
    partners = ((east, lat), (west, lat), (lon, north), (lon, south), (east, south), (west, north))
    for partner in partners:
        pl.semaphore_signal(barrier, inc=1, device_id=partner, device_id_type=MESH)
    fill_bias(raw_ref, bias_ref)
    wk_ref[...] = pltpu.roll(wqkv_ref[:, 128:384].astype(F32), 192, 1).astype(BF)
    qkv_ref[:, 704:768] = jnp.zeros((6 * WIN, 64), BF)
    pl.semaphore_wait(barrier, len(partners))

    def remote(n, src, dst, target):
        return pltpu.make_async_remote_copy(
            src_ref=src, dst_ref=dst, send_sem=send_sem.at[n], recv_sem=recv_sem.at[n],
            device_id=target, device_id_type=MESH,
        )

    halo = [
        remote(0, x_ref.at[:, 3:39, 0:8], from_right, (west, lat)),
        remote(1, x_ref.at[:, 39:72, 16:24], from_left.at[:, 0:33], (east, lat)),
        remote(2, x_ref.at[:, 0:3], near, (lon, south)),
        remote(3, x_ref.at[:, 0:3, 16:24], from_left.at[:, 33:36], (east, south)),
    ]
    home_east = [
        remote(4 + j, to_right.at[:, 12 * j : 12 * j + 12], back_left.at[:, 12 * j : 12 * j + 12], (east, lat))
        for j in range(3)
    ]
    home_west = [
        remote(7 + j, to_left.at[:, 12 * j : end], back_right.at[:, 12 * j : end], (west, lat))
        for j, end in enumerate((12, 24, 33))
    ]
    home_diag = remote(10, to_left.at[:, 33:36], back_diag, (west, north))
    home_lat = remote(11, o_ref.at[:, 72:75], back_lat, (lon, north))
    for copy in halo:
        copy.start()

    def step(s, _):
        phase = s // 3
        turn = lax.rem(s, 3)
        j = jnp.where(phase < 2, turn, 5 - turn)
        inner = (phase == 0) | (phase == 3)

        @pl.when(s == 3)
        def _():
            halo[0].wait_recv()

        @pl.when(s == 6)
        def _():
            for copy in halo[1:]:
                copy.wait_recv()

        def places(last=None):
            for w in range(6):
                for i in range(2):
                    for r in range(6):
                        if last is not None and last != (w % 2 == 1 and r >= 3):
                            continue
                        level = (w // 2 * 2 + 1 + i) % 6
                        row = 3 + 6 * (2 * j + w % 2) + r
                        yield level, row, w * WIN + (i * 6 + r) * 12, r - 3

        def load_inner(level, row, at, source):
            xs[at : at + 12, :] = source[level, row].astype(F32)[6:18]

        def load_left(level, row, at, source):
            xs[at + 6 : at + 12, :] = source[level, row, 0:8].astype(F32)[0:6]

        for wanted, load in ((inner, load_inner), (phase == 2, load_left)):
            @pl.when(wanted)
            def _(load=load):
                for level, row, at, _ in places(False):
                    load(level, row, at, x_ref)

            @pl.when(wanted & (j < 5))
            def _(load=load):
                for level, row, at, _ in places(True):
                    load(level, row, at, x_ref)

            @pl.when(wanted & (j == 5))
            def _(load=load):
                for level, _, at, extra in places(True):
                    load(level, extra, at, near)

        @pl.when(phase == 1)
        def _():
            for level, row, at, _ in places():
                xs[at : at + 6, :] = x_ref[level, row, 16:24].astype(F32)[2:8]
                xs[at + 6 : at + 12, :] = from_right[level, row - 3].astype(F32)[0:6]

        @pl.when(phase == 2)
        def _():
            for level, row, at, _ in places():
                xs[at : at + 6, :] = from_left[level, row - 39].astype(F32)[2:8]

        lat_edge = ((j == 5) & (lat == n_lat - 1)).astype(jnp.int32)
        variants = [w // 4 + (2 * lat_edge if w % 2 else 0) for w in range(6)]
        attend(
            xs, qkv_ref, s_ref, p_ref, ctx_ref, bias_ref, variants,
            g1_ref, wqkv_ref, wk_ref, wp_ref, g2_ref, wup_ref, wdnt_ref,
        )

        @pl.when(inner)
        def _():
            for level, row, at, _ in places():
                o_ref[level, row, 6:18, :] = xs[at : at + 12, :].astype(BF)

        @pl.when(phase == 1)
        def _():
            for level, row, at, _ in places():
                o_ref[level, row, 18:24, :] = xs[at : at + 6, :].astype(BF)
                to_right[level, row - 3, 0:6, :] = xs[at + 6 : at + 12, :].astype(BF)

        @pl.when(phase == 2)
        def _():
            for level, row, at, _ in places():
                to_left[level, row - 39, 2:8, :] = xs[at : at + 6, :].astype(BF)
                o_ref[level, row, 0:6, :] = xs[at + 6 : at + 12, :].astype(BF)

        for n in range(3):
            @pl.when(s == 3 + n)
            def _(n=n):
                home_east[n].start()

            @pl.when(s == 6 + n)
            def _(n=n):
                home_west[2 - n].start()
                if n == 0:
                    home_diag.start()

        @pl.when(s == 9)
        def _():
            home_lat.start()

        return 0

    lax.fori_loop(0, 12, step, 0)
    for copy in home_east:
        copy.wait_recv()
    home_lat.wait_recv()
    home_diag.wait_recv()
    for copy in home_west:
        copy.wait_recv()

    def merge(level, _):
        for r in range(36):
            o_ref[level, 3 + r, 0:6, :] = back_left[level, r, 0:6, :]
        for r in range(33):
            o_ref[level, 39 + r, 18:24, :] = back_right[level, r, 2:8, :]
        for r in range(3):
            o_ref[level, r, 0:18, :] = back_lat[level, r, 0:18, :]
            o_ref[level, r, 18:24, :] = back_diag[level, r, 2:8, :]
        return 0

    lax.fori_loop(0, 6, merge, 0)
    for copy in (*halo, *home_east, *home_west, home_diag, home_lat):
        copy.wait_send()


def block(stream, position_bias, g1, wqkv, wp, g2, wup, wdn):
    vm = pl.BlockSpec(memory_space=pltpu.VMEM)
    slab = pltpu.VMEM((6, 36, 8, D), BF)
    out = pl.pallas_call(
        block_kernel,
        in_specs=[vm] * 8,
        out_specs=vm,
        out_shape=jax.ShapeDtypeStruct((6, 75, 24, D), BF),
        scratch_shapes=[
            pltpu.VMEM((6, 3, 24, D), BF),
            slab, slab, slab, slab,
            slab, pltpu.VMEM((6, 33, 8, D), BF),
            pltpu.VMEM((6, 3, 24, D), BF), pltpu.VMEM((6, 3, 8, D), BF),
            pltpu.VMEM((6 * WIN, D), F32),
            pltpu.VMEM((6 * WIN, 768), BF),
            pltpu.VMEM((2, HEADS * WIN, WIN), F32),
            pltpu.VMEM((2, HEADS * WIN, WIN), BF),
            pltpu.VMEM((6 * WIN, 256), BF),
            pltpu.VMEM((4, HEADS * WIN, WIN), F32),
            pltpu.VMEM((D, 256), BF),
            pltpu.SemaphoreType.DMA((12,)),
            pltpu.SemaphoreType.DMA((12,)),
        ],
        compiler_params=pltpu.CompilerParams(
            collective_id=0, has_side_effects=True, vmem_limit_bytes=32 << 20
        ),
    )(stream, position_bias.reshape(HEADS * WIN, WIN), g1.reshape(1, D), wqkv, wp, g2.reshape(1, D), wup, wdn.T)
    return out[:, :72]


def on_device(
    tokens,
    obs_values,
    obs_dest,
    obs_cell,
    obs_count,
    w_obs,
    ln1_gain,
    w_qkv,
    position_bias,
    w_proj,
    ln2_gain,
    w_up,
    w_down,
):
    received = ship(obs_dest, obs_cell, obs_count, obs_values, w_obs)
    stream = scatter(received, tokens)
    return block(stream, position_bias, ln1_gain, w_qkv, w_proj, ln2_gain, w_up, w_down)


def solution(mesh):
    in_specs = (
        P(None, "lat", "lon", None),
        P(("lon", "lat"), None),
        P(("lon", "lat")),
        P(("lon", "lat")),
        P(("lon", "lat")),
        P(),
        P(),
        P(),
        P(),
        P(),
        P(),
        P(),
        P(),
    )
    out_specs = P(None, "lat", "lon", None)
    return jax.shard_map(
        on_device, mesh=mesh, in_specs=in_specs, out_specs=out_specs, check_vma=False
    )
```
